32 devices in a mesh: pat: 4 (over z), vox: 8 (over y, x, core).
Axes of the slice: x: 2, y: 2, z: 4, core: 2. Of those that a mesh axis runs over, the one named last changes fastest.
Arguments:
- conductivity: float32 [16, 128, 128], P('vox'), may hold values from 0.3 to 1.5
- warm_forward: float32 [16, 32, 128, 128], P('vox', 'pat'), may hold values from -3 to 3
- warm_adjoint: float32 [16, 32, 128, 128], P('vox', 'pat'), may hold values from -3 to 3
- electrodes: int32 [128], replicated, may hold values from 0 to 262143
- patterns: int32 [32, 4], P('pat'), may hold values from 0 to 127, all different within a row
- observed: float32 [32], P('pat'), may hold values from -16 to 16
Outputs:
- gradient: float32 [16, 128, 128], P('vox')
- predicted: float32 [32], P('pat')
The draws below stay inside these ranges and needn't reach their ends.
All inputs are finite; a program needn't handle non-finite values.
Results may differ from the reference program's by a relative error of at most 0.0003.
Values sent between devices are 32-bit elements; how exact they have to be, the bound alone decides.
No kernel may reach another device: no remote copies, remote signals or barrier semaphores. Data moves between devices by JAX's collectives and lax.ppermute only.
A program may use at most 64 MiB of HBM per device.

```python
import math
import jax
import jax.numpy as jnp
from jax import lax

GRID = 128
ELEC = 128
ITERS = 2
NZ = 16
PATTERNS = 32


def warm_potential(key):
    field_shape = (NZ, PATTERNS, GRID, GRID)
    height = 1.0 + 2.0 * jnp.arange(NZ, dtype=jnp.float32)[:, None, None, None] / max(NZ - 1, 1)
    baseline = jnp.clip(jax.random.normal(key, field_shape, jnp.float32), -4.0, 4.0)
    return 0.25 * baseline * height


def draw_warm_forward(key, part):
    return warm_potential(jax.random.fold_in(key, 21))


def draw_warm_adjoint(key, part):
    return warm_potential(jax.random.fold_in(key, 37))


def draw_electrodes(key, part):
    key_depth, key_rows, key_columns = jax.random.split(jax.random.fold_in(key, 11), 3)
    electrode_number = jnp.arange(ELEC, dtype=jnp.int32)
    cycle_depth = electrode_number * NZ // ELEC + jax.random.randint(key_depth, (ELEC,), 0, max(NZ // ELEC, 1))
    row_pick = jax.random.randint(key_rows, (ELEC,), 0, GRID)
    column_pick = jax.random.randint(key_columns, (ELEC,), 0, GRID)
    return ((cycle_depth * GRID + row_pick) * GRID + column_pick).astype(jnp.int32)


def steps_of(rng, dims, cuts, smallest, largest):
    gain = 1.0
    for axis_at, shards_of in cuts:
        heights = jax.random.uniform(jax.random.fold_in(jax.random.fold_in(rng, 6), axis_at), (shards_of,), jnp.float32, smallest / len(cuts), largest / len(cuts))
        gain = gain * jnp.repeat(jnp.exp(heights), dims[axis_at] // shards_of).reshape((-1,) + (1,) * (len(dims) - 1 - axis_at))
    return gain


def different_ones(key, rows, amount, top, lift):
    ranking = jax.random.permutation(jax.random.fold_in(key, 1), amount)
    favour = ranking
    for power in range(3):
        favour = favour * favour // amount
    favour = favour * lift // amount
    lots = jax.random.randint(jax.random.fold_in(key, 2), (rows, amount), 0, 4096) + favour
    sure = jax.random.permutation(jax.random.fold_in(key, 3), rows)[jnp.arange(amount) % rows]
    lots = jnp.where(jnp.arange(rows)[:, None] == sure[None, :], 1 << 14, lots)
    score = lots * amount + jnp.arange(amount)
    return lax.top_k(score.astype(jnp.int32), top)[1].astype(jnp.int32)


def centred(stream_key, shape, scale, most, cuts=(), kind=jnp.bfloat16):
    values = scale * jax.random.normal(stream_key, shape, jnp.float32)
    if cuts:
        values = values * steps_of(stream_key, shape, cuts, -0.22, 0.18)
    return jnp.clip(values, -most, most).astype(kind)


def setup_inputs(seed: int = 0) -> dict:
    splits = jax.random.split(jax.random.key(seed), 7)
    conductivity = jnp.clip(jnp.exp(math.log(1.5) - 1.60943787 * jax.random.uniform(splits[0], (NZ, GRID, GRID), jnp.float32) ** steps_of(splits[0], (NZ, GRID, GRID), ((0, 8),), -0.2, 0.2)), 0.3, 1.5)
    warm_forward = draw_warm_forward(jax.random.fold_in(splits[6], 71), 0)
    warm_adjoint = draw_warm_adjoint(jax.random.fold_in(splits[6], 71), 0)
    electrodes = draw_electrodes(jax.random.fold_in(splits[6], 71), 0)
    patterns = different_ones(splits[4], PATTERNS, ELEC, 4, 0)
    observed = centred(splits[5], (PATTERNS,), 4.0, 16.0, ((0, 4),), jnp.float32)
    return {"conductivity": conductivity, "warm_forward": warm_forward, "warm_adjoint": warm_adjoint, "electrodes": electrodes, "patterns": patterns, "observed": observed}


leakage = 0.05

def both_sides(values, along_axis):
    lower_pad = [(0, 0)] * values.ndim
    upper_pad = [(0, 0)] * values.ndim
    lower_pad[along_axis] = (1, 0)
    upper_pad[along_axis] = (0, 1)
    return jnp.pad(values, lower_pad) + jnp.pad(values, upper_pad)

def spread(values, along_axis):
    lower_pad = [(0, 0)] * values.ndim
    upper_pad = [(0, 0)] * values.ndim
    lower_pad[along_axis] = (1, 0)
    upper_pad[along_axis] = (0, 1)
    return jnp.pad(values, lower_pad) - jnp.pad(values, upper_pad)

def operate(values, coeffs):
    depth_faces, row_faces, column_faces = coeffs
    result = leakage * values
    result = result + spread(depth_faces * (values[1:] - values[:-1]), 0)
    result = result + spread(row_faces * (values[:, 1:] - values[:, :-1]), 1)
    result = result + spread(column_faces * (values[:, :, 1:] - values[:, :, :-1]), 2)
    return result

def solve(right_side, initial, coeffs, diagonal):
    solution = initial
    residue = right_side - operate(solution, coeffs)
    precond = residue / diagonal
    direction = precond
    current = jnp.sum(residue * precond)
    for iteration in range(ITERS):
        applied = operate(direction, coeffs)
        step_size = current / jnp.sum(direction * applied)
        solution = solution + step_size * direction
        residue = residue - step_size * applied
        if iteration + 1 < ITERS:
            precond = residue / diagonal
            following = jnp.sum(residue * precond)
            direction = precond + following / current * direction
            current = following
    return solution

def face_products(forward, adjoint):
    depth_products = (forward[1:] - forward[:-1]) * (adjoint[1:] - adjoint[:-1])
    row_products = (forward[:, 1:] - forward[:, :-1]) * (adjoint[:, 1:] - adjoint[:, :-1])
    column_products = (forward[:, :, 1:] - forward[:, :, :-1]) * (adjoint[:, :, 1:] - adjoint[:, :, :-1])
    return -0.5 * (both_sides(depth_products, 0) + both_sides(row_products, 1) + both_sides(column_products, 2))

def reference(conductivity, warm_forward, warm_adjoint, electrodes, patterns, observed):
    depth_faces = 0.5 * (conductivity[1:] + conductivity[:-1])
    row_faces = 0.5 * (conductivity[:, 1:] + conductivity[:, :-1])
    column_faces = 0.5 * (conductivity[:, :, 1:] + conductivity[:, :, :-1])
    coeffs = (depth_faces, row_faces, column_faces)
    diagonal = leakage + both_sides(depth_faces, 0) + both_sides(row_faces, 1) + both_sides(column_faces, 2)
    voxels = electrodes[patterns].astype(jnp.int32)
    cell_total = NZ * GRID * GRID
    strength = 2.0 * math.sqrt(cell_total)
    data_weight = 0.1 * strength

    def one_pattern(accumulated, pattern_number):
        start_forward = lax.dynamic_index_in_dim(warm_forward, pattern_number, 1, keepdims=False)
        start_adjoint = lax.dynamic_index_in_dim(warm_adjoint, pattern_number, 1, keepdims=False)
        chosen = lax.dynamic_index_in_dim(voxels, pattern_number, 0, keepdims=False)
        right_side = jnp.zeros((cell_total,), jnp.float32).at[chosen[0]].add(strength).at[chosen[1]].add(-strength)
        forward = solve(right_side.reshape(NZ, GRID, GRID), start_forward, coeffs, diagonal)
        flattened = forward.reshape(-1)
        voltage = flattened[chosen[2]] - flattened[chosen[3]]
        misfit = voltage - lax.dynamic_index_in_dim(observed, pattern_number, 0, keepdims=False)
        weighted = data_weight * misfit
        source = jnp.zeros((cell_total,), jnp.float32).at[chosen[2]].add(weighted).at[chosen[3]].add(-weighted)
        adjoint = solve(source.reshape(NZ, GRID, GRID), start_adjoint, coeffs, diagonal)
        return (accumulated + face_products(forward, adjoint), voltage)
    gradient, predicted = lax.scan(one_pattern, jnp.zeros((NZ, GRID, GRID), jnp.float32), jnp.arange(PATTERNS, dtype=jnp.int32))
    return (gradient, predicted)
```

```python
import functools
import math

import jax
import jax.numpy as jnp
from jax import lax
from jax.experimental import pallas as pl
from jax.experimental.pallas import tpu as pltpu
from jax.sharding import PartitionSpec as P

ITERS = 2


leakage = 0.05

CORES = 2
SPARE = 8

VMEM = pl.BlockSpec(memory_space=pltpu.VMEM)
SMEM = pl.BlockSpec(memory_space=pltpu.SMEM)


def call(body, out_shape, scratch=(), smem=0, smem_out=0, operands=()):
    single = not isinstance(out_shape, (tuple, list))
    outs = [out_shape] if single else list(out_shape)
    specs = [VMEM] * (len(outs) - smem_out) + [SMEM] * smem_out
    moved = sum(4 * a.size for a in operands) + sum(4 * o.size for o in outs)
    return pl.pallas_call(
        body,
        out_shape=outs[0] if single else outs,
        in_specs=[SMEM] * smem + [VMEM] * (len(operands) - smem),
        out_specs=specs[0] if single else specs,
        scratch_shapes=list(scratch),
        cost_estimate=pl.CostEstimate(flops=8 * moved, bytes_accessed=moved, transcendentals=0),
    )(*operands)


def shape(*dims):
    return jax.ShapeDtypeStruct(dims, jnp.float32)


def total(acc):
    return jnp.sum(acc, keepdims=True)


def fold(plane):
    rows, columns = plane.shape
    return jnp.sum(plane.reshape(rows // 8, 8, columns), axis=0)


def ahead(plane, axis):
    return pltpu.roll(plane, plane.shape[axis] - 1, axis)


def behind(plane, axis):
    return pltpu.roll(plane, 1, axis)


def split_kernel(place, forward, adjoint, forward_out, adjoint_out):
    chips = forward_out.shape[1]
    first = (1 - place[1]) * chips
    forward_out[...] = forward[:, pl.ds(first, chips)]
    adjoint_out[...] = adjoint[:, pl.ds(first, chips)]


def pack_kernel(place, field, got, *outs):
    chips = len(outs)
    planes = field.shape[0]
    chip, core = place[0], place[1]
    for step, out in enumerate(outs):
        other = chip ^ step
        for plane in range(planes):
            out[core * planes + plane] = field[plane, core * chips + other]
            out[(1 - core) * planes + plane] = got[plane, other]


def coefficient_kernel(place, own, others, depth, rows, columns, inverse, sigma):
    chips, planes = own.shape[:2]
    chip, core = place[0], place[1]
    per_chip = CORES * planes
    for step in range(chips):
        base = (chip ^ step) * per_chip
        for plane in range(planes):
            sigma[base + core * planes + plane] = own[step, plane]
            sigma[base + (1 - core) * planes + plane] = others[step, plane]
    count, height, width = sigma.shape
    row_open = lax.broadcasted_iota(jnp.int32, (height, width), 0) < height - 1
    column_open = lax.broadcasted_iota(jnp.int32, (height, width), 1) < width - 1

    def step(level, below):
        here = sigma[level]
        above = sigma[jnp.minimum(level + 1, count - 1)]
        face_depth = jnp.where(level < count - 1, 0.5, 0.0) * (here + above)
        face_row = jnp.where(row_open, 0.5 * (here + ahead(here, 0)), 0.0)
        face_column = jnp.where(column_open, 0.5 * (here + ahead(here, 1)), 0.0)
        depth[level] = face_depth
        rows[level] = face_row
        columns[level] = face_column
        diagonal = (
            leakage
            + (below + face_depth)
            + (face_row + behind(face_row, 0))
            + (face_column + behind(face_column, 1))
        )
        inverse[level] = 1.0 / diagonal
        return face_depth

    lax.fori_loop(0, count, step, jnp.zeros((height, width), jnp.float32))


def applied_planes(vector, depth, rows, columns, body, start):
    count, height, width = vector.shape

    def step(level, carry):
        here, below, rest = carry
        above = vector[jnp.minimum(level + 1, count - 1)]
        flux_depth = depth[level] * (above - here)
        flux_row = rows[level] * (ahead(here, 0) - here)
        flux_column = columns[level] * (ahead(here, 1) - here)
        result = leakage * here + (below - flux_depth)
        result = result + (behind(flux_row, 0) - flux_row)
        result = result + (behind(flux_column, 1) - flux_column)
        return above, flux_depth, body(level, here, result, rest)

    zero = jnp.zeros((height, width), jnp.float32)
    return lax.fori_loop(0, count, step, (vector[0], zero, start))[2]


def add_at(ref, cell, value):
    count, height, width = ref.shape
    column = cell % width
    row = (cell // width) % height
    level = cell // (width * height)
    lane = lax.broadcasted_iota(jnp.int32, (1, width), 1)
    ref[level, pl.ds(row, 1), :] += jnp.where(lane == column, value, 0.0)


def value_at(ref, cell):
    count, height, width = ref.shape
    column = cell % width
    row = (cell // width) % height
    level = cell // (width * height)
    lane = lax.broadcasted_iota(jnp.int32, (1, width), 1)
    return total(jnp.where(lane == column, ref[level, pl.ds(row, 1), :], 0.0))


def gather_blocks(chip, blocks, field):
    for step, block in enumerate(blocks):
        field[pl.ds((chip ^ step) * block.shape[0], block.shape[0])] = block[...]


def solve_in_place(field, depth, rows, columns, inverse, residue, precond, applied, direction, end):
    count, height, width = field.shape
    nothing = jnp.zeros((8, width), jnp.float32)

    def first(level, here, product, acc):
        left = residue[level] - product
        scaled = left * inverse[level]
        residue[level] = left
        precond[level] = scaled
        return acc + fold(left * scaled)

    current = total(applied_planes(field, depth, rows, columns, first, nothing))

    def second(level, here, product, acc):
        applied[level] = product
        return acc + fold(here * product)

    step_size = current / total(applied_planes(precond, depth, rows, columns, second, nothing))

    def third(level, acc):
        left = residue[level] - step_size * applied[level]
        scaled = left * inverse[level]
        direction[level] = scaled
        return acc + fold(left * scaled)

    following = total(lax.fori_loop(0, count, third, nothing))
    ratio = following / current

    def fourth(level, carry):
        before, acc = carry
        here = direction[level] + ratio * precond[level]
        direction[level] = here
        along_depth = here - before
        along_row = ahead(here, 0) - here
        along_column = ahead(here, 1) - here
        face_depth = jnp.where(level > 0, depth[jnp.maximum(level - 1, 0)], 0.0)
        terms = leakage * here * here + face_depth * along_depth * along_depth
        terms = terms + rows[level] * along_row * along_row
        terms = terms + columns[level] * along_column * along_column
        return here, acc + fold(terms)

    zero = jnp.zeros((height, width), jnp.float32)
    energy = total(lax.fori_loop(0, count, fourth, (zero, nothing))[1])
    last_size = following / energy

    def fifth(level, carry):
        end(level, field[level] + step_size * precond[level] + last_size * direction[level])
        return carry

    lax.fori_loop(0, count, fifth, 0)


def electrode(place, electrodes, patterns, which):
    return electrodes[patterns[place[2], which]]


def clear(ref):
    def step(level, carry):
        ref[level] = jnp.zeros(ref.shape[1:], ref.dtype)
        return carry

    lax.fori_loop(0, ref.shape[0], step, 0)


def forward_kernel(
    strength, chips, place, electrodes, patterns, *refs
):
    depth, rows, columns, inverse = refs[:4]
    blocks = refs[4 : 4 + chips]
    result, voltage, field, residue, precond, applied, direction = refs[4 + chips :]
    gather_blocks(place[0], blocks, field)
    clear(residue)
    add_at(residue, electrode(place, electrodes, patterns, 0), strength)
    add_at(residue, electrode(place, electrodes, patterns, 1), -strength)

    def end(level, plane):
        result[level] = plane

    solve_in_place(
        field, depth, rows, columns, inverse, residue, precond, applied, direction, end
    )
    plus = value_at(result, electrode(place, electrodes, patterns, 2))
    minus = value_at(result, electrode(place, electrodes, patterns, 3))
    voltage[...] = jnp.broadcast_to(plus - minus, voltage.shape)


def adjoint_kernel(
    weight, chips, place, electrodes, patterns, observed, *refs
):
    depth, rows, columns, inverse, forward, voltage = refs[:6]
    blocks = refs[6 : 6 + chips]
    kept, given, field, residue, precond, applied, direction = refs[6 + chips :]
    chip, core = place[0], place[1]
    gather_blocks(chip, blocks, field)
    clear(residue)
    weighted = weight * (voltage[0:1, :] - observed[place[2]])
    add_at(residue, electrode(place, electrodes, patterns, 2), weighted)
    add_at(residue, electrode(place, electrodes, patterns, 3), -weighted)

    def end(level, plane):
        field[level] = plane

    solve_in_place(
        field, depth, rows, columns, inverse, residue, precond, applied, direction, end
    )
    count, height, width = field.shape
    planes = count // (CORES * chips)
    row_open = lax.broadcasted_iota(jnp.int32, (height, width), 0) < height - 1
    column_open = lax.broadcasted_iota(jnp.int32, (height, width), 1) < width - 1

    def step(level, below):
        left, right = forward[level], field[level]
        above = jnp.minimum(level + 1, count - 1)
        product_depth = (forward[above] - left) * (field[above] - right)
        product_row = (ahead(left, 0) - left) * (ahead(right, 0) - right)
        product_row = jnp.where(row_open, product_row, 0.0)
        product_column = (ahead(left, 1) - left) * (ahead(right, 1) - right)
        product_column = jnp.where(column_open, product_column, 0.0)
        plane = -0.5 * (
            (below + product_depth)
            + (product_row + behind(product_row, 0))
            + (product_column + behind(product_column, 1))
        )
        block = (level // (CORES * planes)) ^ chip
        owner = (level // planes) % CORES
        start = pl.multiple_of((level % planes) * height, height)

        @pl.when(owner == core)
        def _():
            kept[block, pl.ds(start, height), :] = plane

        @pl.when(owner != core)
        def _():
            given[block, pl.ds(start, height), :] = plane

        return product_depth

    lax.fori_loop(0, count, step, jnp.zeros((height, width), jnp.float32))
    lane = lax.broadcasted_iota(jnp.int32, (SPARE, width), 1)
    note = jnp.where(lane == place[2], voltage[...], 0.0)
    for block in range(chips):
        kept[block, planes * height :, :] = note
        given[block, planes * height :, :] = note


def swap(values, axis, size, bit):
    return lax.ppermute(values, axis, [(i, i ^ bit) for i in range(size)])


def per_device_exchanged(
    conductivity, warm_forward, warm_adjoint, electrodes, patterns, observed
):
    plane_count, pattern_count, row_count, column_count = warm_forward.shape
    layers = lax.axis_size("vox")
    groups = lax.axis_size("pat")
    chips = layers // CORES
    strength = 2.0 * math.sqrt(layers * plane_count * row_count * column_count)
    position = lax.axis_index("vox")
    chip, core = position // CORES, position % CORES
    place = jnp.stack([chip, core, core * chips + chip]).astype(jnp.int32)
    levels = layers * plane_count
    whole = (levels, row_count, column_count)

    sigma = [conductivity] + [
        swap(conductivity, "vox", layers, CORES * step) for step in range(1, chips)
    ]
    half = shape(plane_count, chips, row_count, column_count)
    give_forward, give_adjoint = call(
        split_kernel, [half, half], smem=1, operands=(place, warm_forward, warm_adjoint)
    )

    def exchanged(field, give):
        got = swap(give, "vox", layers, 1)
        part = shape(CORES * plane_count, row_count, column_count)
        packed = call(pack_kernel, [part] * chips, smem=1, operands=(place, field, got))
        return [packed[0]] + [
            swap(packed[step], "vox", layers, CORES * step) for step in range(1, chips)
        ]

    forward_blocks = exchanged(warm_forward, give_forward)
    adjoint_blocks = exchanged(warm_adjoint, give_adjoint)
    own_sigma = jnp.stack(sigma)
    other_sigma = swap(own_sigma, "vox", layers, 1)
    coefficients = call(
        coefficient_kernel,
        [shape(*whole)] * 4,
        scratch=[pltpu.VMEM(whole, jnp.float32)],
        smem=1,
        operands=(place, own_sigma, other_sigma),
    )
    scratch = [pltpu.VMEM(whole, jnp.float32)] * 5
    forward, voltage = call(
        functools.partial(forward_kernel, strength, chips),
        [shape(*whole), shape(SPARE, column_count)],
        scratch=scratch,
        smem=3,
        operands=(place, electrodes, patterns, *coefficients, *forward_blocks),
    )
    block = plane_count * row_count + SPARE
    kept, given = call(
        functools.partial(adjoint_kernel, 0.1 * strength, chips),
        [shape(chips, block, column_count)] * 2,
        scratch=scratch,
        smem=4,
        operands=(
            place, electrodes, patterns, observed, *coefficients, forward, voltage, *adjoint_blocks
        ),
    )
    summed = kept + swap(given, "vox", layers, 1)
    mine = summed[0]
    for step in range(1, chips):
        mine = mine + swap(summed[step], "vox", layers, CORES * step)
    predicted = mine[plane_count * row_count, :pattern_count]
    gradient = mine[: plane_count * row_count].reshape(plane_count, row_count, column_count)
    bit = 1
    while bit < groups:
        gradient = gradient + swap(gradient, "pat", groups, bit)
        bit *= 2
    return gradient, predicted


def extended(block, sides, width):
    for axis, dim in sides:
        count = lax.axis_size(axis)
        forward = [(i, i + 1) for i in range(count - 1)]
        backward = [(target, source) for source, target in forward]
        low = lax.ppermute(
            lax.slice_in_dim(block, block.shape[dim] - width, None, axis=dim), axis, forward
        )
        high = lax.ppermute(lax.slice_in_dim(block, 0, width, axis=dim), axis, backward)
        block = jnp.concatenate([low, block, high], axis=dim)
    return block


def both_sides(values, along_axis):
    lower_pad = [(0, 0)] * values.ndim
    upper_pad = [(0, 0)] * values.ndim
    lower_pad[along_axis] = (1, 0)
    upper_pad[along_axis] = (0, 1)
    return jnp.pad(values, lower_pad) + jnp.pad(values, upper_pad)


def spread(values, along_axis):
    lower_pad = [(0, 0)] * values.ndim
    upper_pad = [(0, 0)] * values.ndim
    lower_pad[along_axis] = (1, 0)
    upper_pad[along_axis] = (0, 1)
    return jnp.pad(values, lower_pad) - jnp.pad(values, upper_pad)


def operate(values, coeffs):
    depth_faces, row_faces, column_faces = coeffs
    padded = extended(values, (("vox", 0),), 1)
    flux_depth = depth_faces[:, None] * (padded[1:] - padded[:-1])
    result = leakage * values + (flux_depth[:-1] - flux_depth[1:])
    result = result + spread(row_faces[:, None] * (values[:, :, 1:] - values[:, :, :-1]), 2)
    result = result + spread(
        column_faces[:, None] * (values[:, :, :, 1:] - values[:, :, :, :-1]), 3
    )
    return result


def inner(left_factor, right_factor):
    return jnp.sum(left_factor * right_factor, axis=(0, 2, 3))


def widen(vector):
    return vector[None, :, None, None]


def pattern_sum(local_terms):
    return lax.psum(local_terms, "vox")


def solve_pattern(right_side, initial, coeffs, diagonal):
    solution = initial
    residue = right_side - operate(solution, coeffs)
    precond = residue / diagonal
    direction = precond
    current = pattern_sum(inner(residue, precond))
    for iteration in range(ITERS):
        applied = operate(direction, coeffs)
        step_size = current / pattern_sum(inner(direction, applied))
        solution = solution + widen(step_size) * direction
        residue = residue - widen(step_size) * applied
        if iteration + 1 < ITERS:
            precond = residue / diagonal
            following = pattern_sum(inner(residue, precond))
            direction = precond + widen(following / current) * direction
            current = following
    return solution


def per_device_in_place(conductivity, warm_forward, warm_adjoint, electrodes, patterns, observed):
    plane_count, pattern_count, row_count, column_count = warm_forward.shape
    position = lax.axis_index("vox")
    layers = lax.axis_size("vox")
    strength = 2.0 * math.sqrt(layers * plane_count * row_count * column_count)
    data_weight = 0.1 * strength
    lower_open = (position > 0).astype(jnp.float32)
    upper_open = (position < layers - 1).astype(jnp.float32)
    padded_sigma = extended(conductivity, (("vox", 0),), 1)
    face_mask = jnp.concatenate(
        [lower_open[None], jnp.ones((plane_count - 1,), jnp.float32), upper_open[None]]
    )
    depth_faces = 0.5 * (padded_sigma[1:] + padded_sigma[:-1]) * face_mask[:, None, None]
    row_faces = 0.5 * (conductivity[:, 1:] + conductivity[:, :-1])
    column_faces = 0.5 * (conductivity[:, :, 1:] + conductivity[:, :, :-1])
    coeffs = (depth_faces, row_faces, column_faces)
    diagonal = (
        leakage
        + (depth_faces[:-1] + depth_faces[1:])
        + both_sides(row_faces, 1)
        + both_sides(column_faces, 2)
    )
    diagonal = diagonal[:, None]
    electrode_ids = jnp.arange(electrodes.shape[0], dtype=jnp.int32)
    picked = jnp.sum(
        jnp.where(
            patterns[:, :, None] == electrode_ids[None, None, :], electrodes[None, None, :], 0
        ),
        axis=2,
    )
    offset = position * (plane_count * row_count * column_count)
    local_cell = picked - offset
    grid_shape = (plane_count, 1, row_count, column_count)
    cell_index = (
        lax.broadcasted_iota(jnp.int32, grid_shape, 0) * row_count
        + lax.broadcasted_iota(jnp.int32, grid_shape, 2)
    ) * column_count + lax.broadcasted_iota(jnp.int32, grid_shape, 3)

    def marker(which_one):
        return (cell_index == local_cell[:, which_one][None, :, None, None]).astype(jnp.float32)

    forward = solve_pattern(strength * (marker(0) - marker(1)), warm_forward, coeffs, diagonal)
    probe_weights = marker(2) - marker(3)
    predicted = lax.psum(inner(probe_weights, forward), "vox")
    misfit = predicted - observed
    adjoint = solve_pattern(
        widen(data_weight * misfit) * probe_weights, warm_adjoint, coeffs, diagonal
    )
    stacked = jnp.concatenate([forward, adjoint], axis=1)
    padded_pair = extended(stacked, (("vox", 0),), 1)
    padded_forward = padded_pair[:, :pattern_count]
    padded_adjoint = padded_pair[:, pattern_count:]
    depth_products = jnp.sum(
        (padded_forward[1:] - padded_forward[:-1]) * (padded_adjoint[1:] - padded_adjoint[:-1]),
        axis=1,
    )
    depth_products = depth_products * face_mask[:, None, None]
    grad_depth = depth_products[:-1] + depth_products[1:]
    row_products = jnp.sum(
        (forward[:, :, 1:] - forward[:, :, :-1]) * (adjoint[:, :, 1:] - adjoint[:, :, :-1]), axis=1
    )
    column_products = jnp.sum(
        (forward[:, :, :, 1:] - forward[:, :, :, :-1])
        * (adjoint[:, :, :, 1:] - adjoint[:, :, :, :-1]),
        axis=1,
    )
    local_gradient = -0.5 * (
        grad_depth + both_sides(row_products, 1) + both_sides(column_products, 2)
    )
    gradient = lax.psum(local_gradient, "pat")
    return (gradient, predicted)


def per_device(conductivity, warm_forward, *rest):
    size = lax.axis_size("vox")
    groups = lax.axis_size("pat")
    exchange = warm_forward.shape[1] == size and size % CORES == 0
    exchange = exchange and size & (size - 1) == 0 and groups & (groups - 1) == 0
    form = per_device_exchanged if exchange else per_device_in_place
    return form(conductivity, warm_forward, *rest)


def solution(mesh):
    in_specs = (
        P("vox", None, None),
        P("vox", "pat", None, None),
        P("vox", "pat", None, None),
        P(),
        P("pat", None),
        P("pat"),
    )
    out_specs = (P("vox", None, None), P("pat"))
    return jax.shard_map(
        per_device, mesh=mesh, in_specs=in_specs, out_specs=out_specs, check_vma=False
    )
```

```python
import functools
import math

import jax
import jax.numpy as jnp
from jax import lax
from jax.experimental import pallas as pl
from jax.experimental.pallas import tpu as pltpu
from jax.sharding import PartitionSpec as P

ITERS = 2


leakage = 0.05

CORES = 2
SPARE = 8
ROWS = 256

VMEM = pl.BlockSpec(memory_space=pltpu.VMEM)
SMEM = pl.BlockSpec(memory_space=pltpu.SMEM)
ANY = pl.BlockSpec(memory_space=pl.ANY)


def call(body, out_shape, operands, in_specs, scratch=(), limit=8):
    moved = sum(4 * a.size for a in operands) + sum(4 * o.size for o in out_shape)
    return pl.pallas_call(
        body,
        out_shape=out_shape,
        in_specs=in_specs,
        out_specs=[VMEM] * len(out_shape),
        scratch_shapes=list(scratch),
        compiler_params=pltpu.CompilerParams(vmem_limit_bytes=limit << 20),
        cost_estimate=pl.CostEstimate(flops=moved, bytes_accessed=moved, transcendentals=0),
    )(*operands)


def shape(*dims):
    return jax.ShapeDtypeStruct(dims, jnp.float32)


def total(acc):
    return jnp.sum(acc, keepdims=True)


def fold(rows):
    return jnp.sum(rows.reshape(rows.shape[0] // 8, 8, rows.shape[1]), axis=0)


def ahead(rows):
    return pltpu.roll(rows, rows.shape[1] - 1, 1)


def behind(rows):
    return pltpu.roll(rows, 1, 1)


def padded(planes, height, width):
    return ((planes + 2) * height, width)


def clear_edges(*refs, height):
    for ref in refs:
        zero = jnp.zeros((height, ref.shape[1]), ref.dtype)
        ref[:height] = zero
        ref[ref.shape[0] - height :] = zero


def each_chunk(rows, height, body, start, size=ROWS):
    size = math.gcd(size, rows)

    def step(index, carry):
        base = pl.multiple_of(height + index * size, math.gcd(size, height))

        def at(ref, offset=0, value=None):
            where = pl.ds(base + offset, size)
            if value is None:
                return ref[where, :]
            ref[where, :] = value

        return body(at, index * size, carry)

    return lax.fori_loop(0, rows // size, step, start)


def neighbours(at, field, depth, rows, columns, height):
    here, column = at(field), at(columns)
    result = at(depth) * at(field, height) + at(depth, -height) * at(field, -height)
    result += at(rows) * at(field, 1)
    result += at(rows, -1) * at(field, -1)
    result += column * ahead(here) + behind(column * here)
    return here, result


def stage_kernel(place, forward, adjoint, *refs):
    outs, sems = refs[:-1], refs[-1]
    own, give = outs[-2], outs[-1]
    sends = outs[:-2]
    chip, core = place[0], place[1]
    planes, chips = own.shape[:2]
    copies = []
    for step, out in enumerate(sends):
        copies.append((forward.at[:, pl.ds(CORES * (chip ^ step), CORES)], out))
    for plane in range(planes):
        for other in range(chips):
            copies.append((adjoint.at[plane, CORES * other + 1 - core], give.at[plane, other]))
            copies.append((adjoint.at[plane, CORES * other + core], own.at[plane, other]))
    started = [
        pltpu.make_async_copy(source, target, sems.at[number])
        for number, (source, target) in enumerate(copies)
    ]
    for copy in started:
        copy.start()
    for copy in started:
        copy.wait()


def pack_kernel(place, own, got, *outs):
    planes = own.shape[0]
    for step, out in enumerate(outs):
        other = place[0] ^ step
        for plane in range(planes):
            out[0, plane] = own[plane, other]
            out[1, plane] = got[plane, other]


def sort_kernel(place, *refs):
    blocks, keep, give = refs[:-2], refs[-2], refs[-1]
    for step, block in enumerate(blocks):
        for plane in range(block.shape[0]):
            keep[step, plane] = block[plane, place[1]]
            give[step, plane] = block[plane, 1 - place[1]]


def plane_rows(place, step, relative, plane, planes, height):
    level = ((place[0] ^ step) * CORES + (place[1] ^ relative)) * planes + plane
    return pl.ds(pl.multiple_of((level + 1) * height, height), height)


def coefficient_kernel(place, own, others, depth, rows, columns, scale, root, sigma):
    chips, planes, height, width = own.shape
    count = chips * CORES * planes
    clear_edges(depth, rows, columns, scale, root, sigma, height=height)
    for step in range(chips):
        for relative, source in enumerate((own, others)):
            for plane in range(planes):
                sigma[plane_rows(place, step, relative, plane, planes, height), :] = source[
                    step, plane
                ]
    row = lax.broadcasted_iota(jnp.int32, (height, width), 0)
    lane = lax.broadcasted_iota(jnp.int32, (height, width), 1)
    row_ahead, row_behind, lane_ahead = row < height - 1, row > 0, lane < width - 1

    def diagonals(at, first, carry):
        level = first // height
        here = at(sigma)
        along_depth = jnp.where(level > 0, 0.5, 0.0) * (here + at(sigma, -height))
        along_depth += jnp.where(level < count - 1, 0.5, 0.0) * (here + at(sigma, height))
        along_row = jnp.where(row_behind, 0.5 * (here + at(sigma, -1)), 0.0)
        along_row += jnp.where(row_ahead, 0.5 * (here + at(sigma, 1)), 0.0)
        face = jnp.where(lane_ahead, 0.5 * (here + ahead(here)), 0.0)
        diagonal = leakage + along_depth + along_row + (behind(face) + face)
        inverse = lax.rsqrt(diagonal)
        inverse = inverse * (1.5 - 0.5 * diagonal * inverse * inverse)
        at(scale, value=inverse)
        at(root, value=diagonal * inverse)
        return carry

    each_chunk(count * height, height, diagonals, 0, height)

    def couplings(at, first, carry):
        here, size = at(sigma), at(scale)
        half = 0.5 * size
        upper = jnp.where(first // height < count - 1, half, 0.0)
        at(depth, value=upper * ((here + at(sigma, height)) * at(scale, height)))
        face = half * ((here + at(sigma, 1)) * at(scale, 1))
        at(rows, value=jnp.where(row_ahead, face, 0.0))
        face = half * ((here + ahead(here)) * ahead(size))
        at(columns, value=jnp.where(lane_ahead, face, 0.0))
        return carry

    each_chunk(count * height, height, couplings, 0, height)


def spot(ref, cell, height):
    width = ref.shape[1]
    lane = lax.broadcasted_iota(jnp.int32, (1, width), 1)
    return pl.ds(height + cell // width, 1), lane == cell % width


def add_at(ref, scale, cell, value, height):
    row, hit = spot(ref, cell, height)
    ref[row, :] += jnp.where(hit, value * scale[row, :], 0.0)


def value_at(ref, cell, height):
    row, hit = spot(ref, cell, height)
    return total(jnp.where(hit, ref[row, :], 0.0))


def solve_in_place(coefficients, sources, field, residue, applied, later, end, height):
    depth, rows, columns, scale = coefficients
    width = field.shape[1]
    size = field.shape[0] - 2 * height
    nothing = jnp.zeros((8, width), jnp.float32)
    clear_edges(field, residue, later, height=height)

    def first(at, index, carry):
        here, sums = neighbours(at, field, depth, rows, columns, height)
        at(residue, value=sums - here)
        return carry

    each_chunk(size, height, first, 0)
    for cell, value in sources:
        add_at(residue, scale, cell, value, height)

    def second(at, index, carry):
        squares, products = carry
        here, sums = neighbours(at, residue, depth, rows, columns, height)
        product = here - sums
        at(applied, value=product)
        return squares + fold(here * here), products + fold(here * product)

    squares, products = each_chunk(size, height, second, (nothing, nothing))
    current, energy = total(squares), total(products)
    step_size = current / energy

    def third(at, index, carry):
        squares, products = carry
        product = at(applied)
        left = at(residue) - step_size * product
        at(later, value=left)
        return squares + fold(left * left), products + fold(left * product)

    squares, products = each_chunk(size, height, third, (nothing, nothing))
    following, cross = total(squares), total(products)
    ratio = following / current

    def fourth(at, index, acc):
        here = at(later)
        sums = at(depth, -height) * at(later, -height) + at(rows, -1) * at(later, -1)
        sums += behind(at(columns) * here)
        return acc + fold(here * (here - 2.0 * sums))

    own = total(each_chunk(size, height, fourth, nothing))
    last_size = following / (own + ratio * (2.0 * cross + ratio * energy))
    first_size = step_size + last_size * ratio

    def fifth(at, index, carry):
        moved = at(field) + first_size * at(residue) + last_size * at(later)
        end(at, at(scale) * moved)
        return carry

    each_chunk(size, height, fifth, 0)


def electrode(place, electrodes, patterns, which):
    return electrodes[patterns[place[2], which]]


def forward_kernel(strength, place, electrodes, patterns, *refs):
    depth, rows, columns, scale, root, own, others = refs[:7]
    result, slopes, voltage, field, residue, applied, later = refs[7:]
    chips, planes, height, width = own.shape
    for step in range(chips):
        for relative, source in enumerate((own, others)):
            for plane in range(planes):
                where = plane_rows(place, step, relative, plane, planes, height)
                field[where, :] = source[step, plane] * root[where, :]
    plus, minus, high, low = (
        electrode(place, electrodes, patterns, which) for which in range(4)
    )
    lane = lax.broadcasted_iota(jnp.int32, (1, width), 1)
    weight = jnp.where(lane < width - 1, -0.5, 0.0)

    def end(at, potential):
        at(result, value=potential)
        at(slopes, value=weight * (ahead(potential) - potential))

    solve_in_place(
        (depth, rows, columns, scale),
        ((plus, strength), (minus, -strength)),
        field, residue, applied, later, end, height,
    )
    clear_edges(result, height=height)
    seen = value_at(result, high, height) - value_at(result, low, height)
    voltage[...] = jnp.broadcast_to(seen, voltage.shape)


def adjoint_kernel(weight, place, electrodes, patterns, observed, *refs):
    depth, rows, columns, scale, root, forward, slopes, voltage = refs[:8]
    *blocks, kept, given, field, residue, applied, later, adjoint = refs[8:]
    chips = len(blocks)
    planes, height, width = blocks[0].shape[1:]
    count = chips * CORES * planes
    for step, block in enumerate(blocks):
        for relative in range(CORES):
            for plane in range(planes):
                where = plane_rows(place, step, relative, plane, planes, height)
                field[where, :] = block[relative, plane] * root[where, :]
    weighted = weight * (voltage[0:1, :] - observed[place[2]])
    high = electrode(place, electrodes, patterns, 2)
    low = electrode(place, electrodes, patterns, 3)

    def end(at, potential):
        at(adjoint, value=potential)

    solve_in_place(
        (depth, rows, columns, scale),
        ((high, weighted), (low, -weighted)),
        field, residue, applied, later, end, height,
    )
    clear_edges(adjoint, height=height)
    row = lax.broadcasted_iota(jnp.int32, (height, 1), 0)
    row_ahead = jnp.where(row < height - 1, -0.5, 0.0)
    row_behind = jnp.where(row > 0, -0.5, 0.0)

    def step(at, first, carry):
        level = first // height
        left, right = at(forward), at(adjoint)

        def product(offset):
            return (at(forward, offset) - left) * (at(adjoint, offset) - right)

        plane = jnp.where(level < count - 1, -0.5, 0.0) * product(height)
        plane += jnp.where(level > 0, -0.5, 0.0) * product(-height)
        plane += row_ahead * product(1) + row_behind * product(-1)
        face = at(slopes) * (ahead(right) - right)
        plane += face + behind(face)
        block = (level // (CORES * planes)) ^ place[0]
        owner = (level // planes) % CORES
        start = pl.multiple_of((level % planes) * height, height)

        @pl.when(owner == place[1])
        def _():
            kept[block, pl.ds(start, height), :] = plane

        @pl.when(owner != place[1])
        def _():
            given[block, pl.ds(start, height), :] = plane

        return carry

    each_chunk(count * height, height, step, 0, height)
    lane = lax.broadcasted_iota(jnp.int32, (SPARE, width), 1)
    note = jnp.where(lane == place[2], voltage[...], 0.0)
    for block in range(chips):
        kept[block, planes * height :, :] = note
        given[block, planes * height :, :] = note


def swap(values, axis, size, bit):
    return lax.ppermute(values, axis, [(i, i ^ bit) for i in range(size)])


def per_device_exchanged(
    conductivity, warm_forward, warm_adjoint, electrodes, patterns, observed
):
    plane_count, pattern_count, row_count, column_count = warm_forward.shape
    layers = lax.axis_size("vox")
    groups = lax.axis_size("pat")
    chips = layers // CORES
    strength = 2.0 * math.sqrt(layers * plane_count * row_count * column_count)
    position = lax.axis_index("vox")
    chip, core = position // CORES, position % CORES
    place = jnp.stack([chip, core, position]).astype(jnp.int32)
    plane = (row_count, column_count)
    whole = shape(*padded(layers * plane_count, *plane))
    room = pltpu.VMEM(whole.shape, jnp.float32)

    def chip_swap(values, step):
        return swap(values, "vox", layers, CORES * step)

    def core_swap(values):
        return swap(values, "vox", layers, 1)

    sigma = [conductivity] + [chip_swap(conductivity, step) for step in range(1, chips)]
    *sends, own, give = call(
        stage_kernel,
        [shape(plane_count, CORES, *plane)] * chips
        + [shape(plane_count, chips, *plane)] * 2,
        (place, warm_forward, warm_adjoint),
        [SMEM, ANY, ANY],
        scratch=[pltpu.SemaphoreType.DMA((chips + 2 * chips * plane_count,))],
    )
    blocks = [sends[0]] + [chip_swap(sends[step], step) for step in range(1, chips)]
    got = core_swap(give)
    packed = call(
        pack_kernel,
        [shape(CORES, plane_count, *plane)] * chips,
        (place, own, got),
        [SMEM, VMEM, VMEM],
    )
    adjoint_blocks = [packed[0]] + [chip_swap(packed[step], step) for step in range(1, chips)]
    own_sigma = jnp.stack(sigma)
    other_sigma = core_swap(own_sigma)
    coefficients = call(
        coefficient_kernel,
        [whole] * 5,
        (place, own_sigma, other_sigma),
        [SMEM, VMEM, VMEM],
        scratch=[room],
        limit=16,
    )
    half = shape(chips, plane_count, *plane)
    keep, pass_on = call(sort_kernel, [half] * 2, (place, *blocks), [SMEM] + [VMEM] * chips)
    received = core_swap(pass_on)
    forward, slopes, voltage = call(
        functools.partial(forward_kernel, strength),
        [whole, whole, shape(SPARE, column_count)],
        (place, electrodes, patterns, *coefficients, keep, received),
        [SMEM] * 3 + [VMEM] * 7,
        scratch=[room] * 4,
        limit=20,
    )
    block = shape(chips, plane_count * row_count + SPARE, column_count)
    kept, given = call(
        functools.partial(adjoint_kernel, 0.1 * strength),
        [block] * 2,
        (
            place, electrodes, patterns, observed,
            *coefficients, forward, slopes, voltage, *adjoint_blocks,
        ),
        [SMEM] * 4 + [VMEM] * (8 + chips),
        scratch=[room] * 5,
        limit=24,
    )
    summed = kept + core_swap(given)
    mine = summed[0]
    for step in range(1, chips):
        mine = mine + chip_swap(summed[step], step)
    predicted = mine[plane_count * row_count, :pattern_count]
    gradient = mine[: plane_count * row_count].reshape(plane_count, *plane)
    bit = 1
    while bit < groups:
        gradient = gradient + swap(gradient, "pat", groups, bit)
        bit *= 2
    return gradient, predicted


def extended(block, sides, width):
    for axis, dim in sides:
        count = lax.axis_size(axis)
        forward = [(i, i + 1) for i in range(count - 1)]
        backward = [(target, source) for source, target in forward]
        low = lax.ppermute(
            lax.slice_in_dim(block, block.shape[dim] - width, None, axis=dim), axis, forward
        )
        high = lax.ppermute(lax.slice_in_dim(block, 0, width, axis=dim), axis, backward)
        block = jnp.concatenate([low, block, high], axis=dim)
    return block


def both_sides(values, along_axis):
    lower_pad = [(0, 0)] * values.ndim
    upper_pad = [(0, 0)] * values.ndim
    lower_pad[along_axis] = (1, 0)
    upper_pad[along_axis] = (0, 1)
    return jnp.pad(values, lower_pad) + jnp.pad(values, upper_pad)


def spread(values, along_axis):
    lower_pad = [(0, 0)] * values.ndim
    upper_pad = [(0, 0)] * values.ndim
    lower_pad[along_axis] = (1, 0)
    upper_pad[along_axis] = (0, 1)
    return jnp.pad(values, lower_pad) - jnp.pad(values, upper_pad)


def operate(values, coeffs):
    depth_faces, row_faces, column_faces = coeffs
    padded = extended(values, (("vox", 0),), 1)
    flux_depth = depth_faces[:, None] * (padded[1:] - padded[:-1])
    result = leakage * values + (flux_depth[:-1] - flux_depth[1:])
    result = result + spread(row_faces[:, None] * (values[:, :, 1:] - values[:, :, :-1]), 2)
    result = result + spread(
        column_faces[:, None] * (values[:, :, :, 1:] - values[:, :, :, :-1]), 3
    )
    return result


def inner(left_factor, right_factor):
    return jnp.sum(left_factor * right_factor, axis=(0, 2, 3))


def widen(vector):
    return vector[None, :, None, None]


def pattern_sum(local_terms):
    return lax.psum(local_terms, "vox")


def solve_pattern(right_side, initial, coeffs, diagonal):
    solution = initial
    residue = right_side - operate(solution, coeffs)
    precond = residue / diagonal
    direction = precond
    current = pattern_sum(inner(residue, precond))
    for iteration in range(ITERS):
        applied = operate(direction, coeffs)
        step_size = current / pattern_sum(inner(direction, applied))
        solution = solution + widen(step_size) * direction
        residue = residue - widen(step_size) * applied
        if iteration + 1 < ITERS:
            precond = residue / diagonal
            following = pattern_sum(inner(residue, precond))
            direction = precond + widen(following / current) * direction
            current = following
    return solution


def per_device_in_place(conductivity, warm_forward, warm_adjoint, electrodes, patterns, observed):
    plane_count, pattern_count, row_count, column_count = warm_forward.shape
    position = lax.axis_index("vox")
    layers = lax.axis_size("vox")
    strength = 2.0 * math.sqrt(layers * plane_count * row_count * column_count)
    data_weight = 0.1 * strength
    lower_open = (position > 0).astype(jnp.float32)
    upper_open = (position < layers - 1).astype(jnp.float32)
    padded_sigma = extended(conductivity, (("vox", 0),), 1)
    face_mask = jnp.concatenate(
        [lower_open[None], jnp.ones((plane_count - 1,), jnp.float32), upper_open[None]]
    )
    depth_faces = 0.5 * (padded_sigma[1:] + padded_sigma[:-1]) * face_mask[:, None, None]
    row_faces = 0.5 * (conductivity[:, 1:] + conductivity[:, :-1])
    column_faces = 0.5 * (conductivity[:, :, 1:] + conductivity[:, :, :-1])
    coeffs = (depth_faces, row_faces, column_faces)
    diagonal = (
        leakage
        + (depth_faces[:-1] + depth_faces[1:])
        + both_sides(row_faces, 1)
        + both_sides(column_faces, 2)
    )
    diagonal = diagonal[:, None]
    electrode_ids = jnp.arange(electrodes.shape[0], dtype=jnp.int32)
    picked = jnp.sum(
        jnp.where(
            patterns[:, :, None] == electrode_ids[None, None, :], electrodes[None, None, :], 0
        ),
        axis=2,
    )
    offset = position * (plane_count * row_count * column_count)
    local_cell = picked - offset
    grid_shape = (plane_count, 1, row_count, column_count)
    cell_index = (
        lax.broadcasted_iota(jnp.int32, grid_shape, 0) * row_count
        + lax.broadcasted_iota(jnp.int32, grid_shape, 2)
    ) * column_count + lax.broadcasted_iota(jnp.int32, grid_shape, 3)

    def marker(which_one):
        return (cell_index == local_cell[:, which_one][None, :, None, None]).astype(jnp.float32)

    forward = solve_pattern(strength * (marker(0) - marker(1)), warm_forward, coeffs, diagonal)
    probe_weights = marker(2) - marker(3)
    predicted = lax.psum(inner(probe_weights, forward), "vox")
    misfit = predicted - observed
    adjoint = solve_pattern(
        widen(data_weight * misfit) * probe_weights, warm_adjoint, coeffs, diagonal
    )
    stacked = jnp.concatenate([forward, adjoint], axis=1)
    padded_pair = extended(stacked, (("vox", 0),), 1)
    padded_forward = padded_pair[:, :pattern_count]
    padded_adjoint = padded_pair[:, pattern_count:]
    depth_products = jnp.sum(
        (padded_forward[1:] - padded_forward[:-1]) * (padded_adjoint[1:] - padded_adjoint[:-1]),
        axis=1,
    )
    depth_products = depth_products * face_mask[:, None, None]
    grad_depth = depth_products[:-1] + depth_products[1:]
    row_products = jnp.sum(
        (forward[:, :, 1:] - forward[:, :, :-1]) * (adjoint[:, :, 1:] - adjoint[:, :, :-1]), axis=1
    )
    column_products = jnp.sum(
        (forward[:, :, :, 1:] - forward[:, :, :, :-1])
        * (adjoint[:, :, :, 1:] - adjoint[:, :, :, :-1]),
        axis=1,
    )
    local_gradient = -0.5 * (
        grad_depth + both_sides(row_products, 1) + both_sides(column_products, 2)
    )
    gradient = lax.psum(local_gradient, "pat")
    return (gradient, predicted)


def per_device(conductivity, warm_forward, *rest):
    size = lax.axis_size("vox")
    groups = lax.axis_size("pat")
    exchange = warm_forward.shape[1] == size and size % CORES == 0
    exchange = exchange and size & (size - 1) == 0 and groups & (groups - 1) == 0
    form = per_device_exchanged if exchange else per_device_in_place
    return form(conductivity, warm_forward, *rest)


def solution(mesh):
    in_specs = (
        P("vox", None, None),
        P("vox", "pat", None, None),
        P("vox", "pat", None, None),
        P(),
        P("pat", None),
        P("pat"),
    )
    out_specs = (P("vox", None, None), P("pat"))
    return jax.shard_map(
        per_device, mesh=mesh, in_specs=in_specs, out_specs=out_specs, check_vma=False
    )
```

```python
import functools
import math

import jax
import jax.numpy as jnp
from jax import lax
from jax.experimental import pallas as pl
from jax.experimental.pallas import tpu as pltpu
from jax.sharding import PartitionSpec as P


ITERS = 2


leakage = 0.05

CORES = 2
SPARE = 8
ROWS = 256


VMEM = pl.BlockSpec(memory_space=pltpu.VMEM)
SMEM = pl.BlockSpec(memory_space=pltpu.SMEM)
HBM = pl.BlockSpec(memory_space=pltpu.HBM)


def call(body, out_shape, operands, in_specs, scratch=(), limit=1):
    moved = sum(4 * a.size for a in operands) + sum(4 * o.size for o in out_shape)
    return pl.pallas_call(
        body,
        out_shape=out_shape,
        in_specs=in_specs,
        out_specs=[VMEM] * len(out_shape),
        scratch_shapes=list(scratch),
        compiler_params=pltpu.CompilerParams(vmem_limit_bytes=limit << 20),
        cost_estimate=pl.CostEstimate(flops=moved, bytes_accessed=moved, transcendentals=0),
    )(*operands)


def shape(*dims):
    return jax.ShapeDtypeStruct(dims, jnp.float32)


def total(acc):
    return jnp.sum(acc, keepdims=True)


def fold(rows):
    return jnp.sum(rows.reshape(rows.shape[0] // 8, 8, rows.shape[1]), axis=0)


def ahead(rows):
    return pltpu.roll(rows, rows.shape[1] - 1, 1)


def behind(rows):
    return pltpu.roll(rows, 1, 1)


def padded(planes, height, width):
    return ((planes + 2) * height, width)


def clear_edges(*refs, height):
    for ref in refs:
        zero = jnp.zeros((height, ref.shape[1]), ref.dtype)
        ref[:height] = zero
        ref[ref.shape[0] - height :] = zero


def each_chunk(rows, height, body, start, size=ROWS):
    size = math.gcd(size, rows)

    def step(index, carry):
        base = pl.multiple_of(height + index * size, math.gcd(size, height))

        def at(ref, offset=0, value=None):
            where = pl.ds(base + offset, size)
            if value is None:
                return ref[where, :]
            ref[where, :] = value

        return body(at, index * size, carry)

    return lax.fori_loop(0, rows // size, step, start)


def neighbours(at, field, depth, rows, columns, height):
    here, column = at(field), at(columns)
    result = at(depth) * at(field, height) + at(depth, -height) * at(field, -height)
    result += at(rows) * at(field, 1)
    result += at(rows, -1) * at(field, -1)
    result += column * ahead(here) + behind(column * here)
    return here, result


def my_place():
    position = lax.axis_index("vox")
    return lax.div(position, CORES), lax.rem(position, CORES), position


def stage_kernel(forward, adjoint, *refs):
    place = my_place()
    outs, sems = refs[:-1], refs[-1]
    own, give = outs[-2], outs[-1]
    sends = outs[:-2]
    chip, core = place[0], place[1]
    planes, chips = own.shape[:2]
    copies = []
    for step, out in enumerate(sends):
        copies.append((forward.at[:, pl.ds(CORES * (chip ^ step), CORES)], out))
    for plane in range(planes):
        for other in range(chips):
            copies.append((adjoint.at[plane, CORES * other + 1 - core], give.at[plane, other]))
            copies.append((adjoint.at[plane, CORES * other + core], own.at[plane, other]))
    started = [
        pltpu.make_async_copy(source, target, sems.at[number])
        for number, (source, target) in enumerate(copies)
    ]
    for copy in started:
        copy.start()
    for copy in started:
        copy.wait()


def pack_kernel(own, got, *outs):
    place = my_place()
    planes = own.shape[0]
    for step, out in enumerate(outs):
        other = place[0] ^ step
        for plane in range(planes):
            out[0, plane] = own[plane, other]
            out[1, plane] = got[plane, other]


def sort_kernel(*refs):
    place = my_place()
    blocks, keep, give = refs[:-2], refs[-2], refs[-1]
    for step, block in enumerate(blocks):
        for plane in range(block.shape[0]):
            keep[step, plane] = block[plane, place[1]]
            give[step, plane] = block[plane, 1 - place[1]]


def plane_rows(place, step, relative, plane, planes, height):
    level = ((place[0] ^ step) * CORES + (place[1] ^ relative)) * planes + plane
    return pl.ds(pl.multiple_of((level + 1) * height, height), height)


def coefficient_kernel(own, others, depth, rows, columns, scale, root, sigma):
    place = my_place()
    chips, planes, height, width = own.shape
    count = chips * CORES * planes
    clear_edges(depth, rows, columns, scale, root, sigma, height=height)
    for step in range(chips):
        for relative, source in enumerate((own, others)):
            for plane in range(planes):
                sigma[plane_rows(place, step, relative, plane, planes, height), :] = source[
                    step, plane
                ]
    row = lax.broadcasted_iota(jnp.int32, (height, width), 0)
    lane = lax.broadcasted_iota(jnp.int32, (height, width), 1)
    row_ahead, row_behind, lane_ahead = row < height - 1, row > 0, lane < width - 1

    def diagonals(at, first, carry):
        level = first // height
        here = at(sigma)
        along_depth = jnp.where(level > 0, 0.5, 0.0) * (here + at(sigma, -height))
        along_depth += jnp.where(level < count - 1, 0.5, 0.0) * (here + at(sigma, height))
        along_row = jnp.where(row_behind, 0.5 * (here + at(sigma, -1)), 0.0)
        along_row += jnp.where(row_ahead, 0.5 * (here + at(sigma, 1)), 0.0)
        face = jnp.where(lane_ahead, 0.5 * (here + ahead(here)), 0.0)
        diagonal = leakage + along_depth + along_row + (behind(face) + face)
        inverse = lax.rsqrt(diagonal)
        inverse = inverse * (1.5 - 0.5 * diagonal * inverse * inverse)
        at(scale, value=inverse)
        at(root, value=diagonal * inverse)
        return carry

    each_chunk(count * height, height, diagonals, 0, height)

    def couplings(at, first, carry):
        here, size = at(sigma), at(scale)
        half = 0.5 * size
        upper = jnp.where(first // height < count - 1, half, 0.0)
        at(depth, value=upper * ((here + at(sigma, height)) * at(scale, height)))
        face = half * ((here + at(sigma, 1)) * at(scale, 1))
        at(rows, value=jnp.where(row_ahead, face, 0.0))
        face = half * ((here + ahead(here)) * ahead(size))
        at(columns, value=jnp.where(lane_ahead, face, 0.0))
        return carry

    each_chunk(count * height, height, couplings, 0, height)


def spot(ref, cell, height):
    width = ref.shape[1]
    lane = lax.broadcasted_iota(jnp.int32, (1, width), 1)
    return pl.ds(height + cell // width, 1), lane == cell % width


def add_at(ref, scale, cell, value, height):
    row, hit = spot(ref, cell, height)
    ref[row, :] += jnp.where(hit, value * scale[row, :], 0.0)


def value_at(ref, cell, height):
    row, hit = spot(ref, cell, height)
    return total(jnp.where(hit, ref[row, :], 0.0))


def solve_in_place(coefficients, sources, field, residue, applied, later, end, height):
    depth, rows, columns, scale = coefficients
    width = field.shape[1]
    size = field.shape[0] - 2 * height
    nothing = jnp.zeros((8, width), jnp.float32)
    clear_edges(field, residue, applied, height=height)

    def first(at, index, carry):
        here, sums = neighbours(at, field, depth, rows, columns, height)
        at(residue, value=sums - here)
        return carry

    each_chunk(size, height, first, 0)
    for cell, value in sources:
        add_at(residue, scale, cell, value, height)

    def second(at, index, carry):
        squares, products = carry
        here, sums = neighbours(at, residue, depth, rows, columns, height)
        product = here - sums
        at(applied, value=product)
        return squares + fold(here * here), products + fold(here * product)

    squares, products = each_chunk(size, height, second, (nothing, nothing))
    current, energy = total(squares), total(products)
    step_size = current / energy

    def third(at, index, carry):
        squares, products, energies = carry

        def left(offset=0):
            return at(residue, offset) - step_size * at(applied, offset)

        here = left()
        at(later, value=here)
        sums = at(depth, -height) * left(-height) + at(rows, -1) * left(-1)
        sums += behind(at(columns) * here)
        squares = squares + fold(here * here)
        products = products + fold(here * at(applied))
        return squares, products, energies + fold(here * (here - 2.0 * sums))

    squares, products, energies = each_chunk(size, height, third, (nothing,) * 3)
    following, cross, own = total(squares), total(products), total(energies)
    ratio = following / current
    last_size = following / (own + ratio * (2.0 * cross + ratio * energy))
    first_size = step_size + last_size * ratio

    def fifth(at, index, carry):
        moved = at(field) + first_size * at(residue) + last_size * at(later)
        end(at, at(scale) * moved)
        return carry

    each_chunk(size, height, fifth, 0)


def electrode(place, electrodes, patterns, which):
    return electrodes[patterns[which, place[2]]]


def forward_kernel(strength, electrodes, patterns, *refs):
    place = my_place()
    depth, rows, columns, scale, root, own, others = refs[:7]
    *slopes, voltage, field, residue, applied, later, result = refs[7:]
    chips, planes, height, width = own.shape
    for step in range(chips):
        for relative, source in enumerate((own, others)):
            for plane in range(planes):
                where = plane_rows(place, step, relative, plane, planes, height)
                field[where, :] = source[step, plane] * root[where, :]
    plus, minus, high, low = (
        electrode(place, electrodes, patterns, which) for which in range(4)
    )

    def end(at, potential):
        at(result, value=potential)

    solve_in_place(
        (depth, rows, columns, scale),
        ((plus, strength), (minus, -strength)),
        field, residue, applied, later, end, height,
    )
    clear_edges(result, *slopes, height=height)
    count = chips * CORES * planes
    row = lax.broadcasted_iota(jnp.int32, (height, 1), 0)
    lane = lax.broadcasted_iota(jnp.int32, (1, width), 1)
    row_weight = jnp.where(row < height - 1, -0.5, 0.0)
    lane_weight = jnp.where(lane < width - 1, -0.5, 0.0)
    along_depth, along_row, along_column = slopes

    def slope(at, first, carry):
        here = at(result)
        depth_weight = jnp.where(first // height < count - 1, -0.5, 0.0)
        at(along_depth, value=depth_weight * (at(result, height) - here))
        at(along_row, value=row_weight * (at(result, 1) - here))
        at(along_column, value=lane_weight * (ahead(here) - here))
        return carry

    each_chunk(count * height, height, slope, 0, height)
    seen = value_at(result, high, height) - value_at(result, low, height)
    voltage[...] = jnp.broadcast_to(seen, voltage.shape)


def adjoint_kernel(weight, electrodes, patterns, observed, *refs):
    place = my_place()
    depth, rows, columns, scale, root, *slopes, voltage = refs[:9]
    *blocks, adjoint, given, field, residue, applied, later = refs[9:]
    planes, height, _ = blocks[0].shape[1:]
    for step, block in enumerate(blocks):
        for relative in range(CORES):
            for plane in range(planes):
                where = plane_rows(place, step, relative, plane, planes, height)
                field[where, :] = block[relative, plane] * root[where, :]
    weighted = weight * (voltage[0:1, :] - observed[place[2]])
    high = electrode(place, electrodes, patterns, 2)
    low = electrode(place, electrodes, patterns, 3)

    def end(at, potential):
        at(adjoint, value=potential)

    solve_in_place(
        (depth, rows, columns, scale),
        ((high, weighted), (low, -weighted)),
        field, residue, applied, later, end, height,
    )
    clear_edges(adjoint, height=height)
    gradient_blocks(place, 1, slopes, voltage, adjoint, given, planes, height)


def gradient_kernel(planes, height, *refs):
    place = my_place()
    *slopes, voltage, adjoint, kept = refs
    gradient_blocks(place, 0, slopes, voltage, adjoint, kept, planes, height)


def gradient_blocks(place, relative, slopes, voltage, adjoint, out, planes, height):
    along_depth, along_row, along_column = slopes
    chips, width = out.shape[0], out.shape[2]
    size = planes * height

    def step(block, carry):
        start = plane_rows(place, block, relative, 0, planes, height).start

        def at(ref, offset=0):
            return ref[pl.ds(start + offset, size), :]

        here = at(adjoint)
        result = at(along_depth) * (at(adjoint, height) - here)
        result += at(along_depth, -height) * (here - at(adjoint, -height))
        result += at(along_row) * (at(adjoint, 1) - here)
        result += at(along_row, -1) * (here - at(adjoint, -1))
        face = at(along_column) * (ahead(here) - here)
        out[block, :size, :] = result + (face + behind(face))
        return carry

    lax.fori_loop(0, chips, step, 0)
    lane = lax.broadcasted_iota(jnp.int32, (SPARE, width), 1)
    note = jnp.where(lane == place[2], voltage[...], 0.0)
    for block in range(chips):
        out[block, size:, :] = note


def swap(values, axis, size, bit):
    return lax.ppermute(values, axis, [(i, i ^ bit) for i in range(size)])


def per_device_exchanged(
    conductivity, warm_forward, warm_adjoint, electrodes, patterns, observed
):
    plane_count, pattern_count, row_count, column_count = warm_forward.shape
    layers = lax.axis_size("vox")
    groups = lax.axis_size("pat")
    chips = layers // CORES
    strength = 2.0 * math.sqrt(layers * plane_count * row_count * column_count)
    plane = (row_count, column_count)
    whole = shape(*padded(layers * plane_count, *plane))
    room = pltpu.VMEM(whole.shape, jnp.float32)

    def chip_swap(values, step):
        return swap(values, "vox", layers, CORES * step)

    def core_swap(values):
        return swap(values, "vox", layers, 1)

    sigma = [conductivity] + [chip_swap(conductivity, step) for step in range(1, chips)]
    *sends, own, give = call(
        stage_kernel,
        [shape(plane_count, CORES, *plane)] * chips
        + [shape(plane_count, chips, *plane)] * 2,
        (
            pltpu.with_memory_space_constraint(warm_forward, pltpu.HBM),
            pltpu.with_memory_space_constraint(warm_adjoint, pltpu.HBM),
        ),
        [HBM, HBM],
        scratch=[pltpu.SemaphoreType.DMA((chips + 2 * chips * plane_count,))],
    )
    blocks = [sends[0]] + [chip_swap(sends[step], step) for step in range(1, chips)]
    got = core_swap(give)
    packed = call(
        pack_kernel, [shape(CORES, plane_count, *plane)] * chips, (own, got), [VMEM, VMEM]
    )
    adjoint_blocks = [packed[0]] + [chip_swap(packed[step], step) for step in range(1, chips)]
    own_sigma = jnp.stack(sigma)
    other_sigma = core_swap(own_sigma)
    coefficients = call(
        coefficient_kernel,
        [whole] * 5,
        (own_sigma, other_sigma),
        [VMEM, VMEM],
        scratch=[room],
        limit=3,
    )
    half = shape(chips, plane_count, *plane)
    keep, pass_on = call(sort_kernel, [half] * 2, tuple(blocks), [VMEM] * chips)
    received = core_swap(pass_on)
    *slopes, voltage = call(
        functools.partial(forward_kernel, strength),
        [whole] * 3 + [shape(SPARE, column_count)],
        (electrodes, patterns.T, *coefficients, keep, received),
        [SMEM] * 2 + [VMEM] * 7,
        scratch=[room] * 5,
        limit=8,
    )
    block = shape(chips, plane_count * row_count + SPARE, column_count)
    adjoint, given = call(
        functools.partial(adjoint_kernel, 0.1 * strength),
        [whole, block],
        (
            electrodes, patterns.T, observed,
            *coefficients, *slopes, voltage, *adjoint_blocks,
        ),
        [SMEM] * 3 + [VMEM] * (9 + chips),
        scratch=[room] * 4,
        limit=8,
    )
    (kept,) = call(
        functools.partial(gradient_kernel, plane_count, row_count),
        [block],
        (*slopes, voltage, adjoint),
        [VMEM] * 5,
    )
    summed = kept + core_swap(given)
    mine = summed[0]
    for step in range(1, chips):
        mine = mine + chip_swap(summed[step], step)
    predicted = mine[plane_count * row_count, :pattern_count]
    gradient = mine[: plane_count * row_count].reshape(plane_count, *plane)
    bit = 1
    while bit < groups:
        gradient = gradient + swap(gradient, "pat", groups, bit)
        bit *= 2
    return gradient, predicted


def extended(block, sides, width):
    for axis, dim in sides:
        count = lax.axis_size(axis)
        forward = [(i, i + 1) for i in range(count - 1)]
        backward = [(target, source) for source, target in forward]
        low = lax.ppermute(
            lax.slice_in_dim(block, block.shape[dim] - width, None, axis=dim), axis, forward
        )
        high = lax.ppermute(lax.slice_in_dim(block, 0, width, axis=dim), axis, backward)
        block = jnp.concatenate([low, block, high], axis=dim)
    return block


def both_sides(values, along_axis):
    lower_pad = [(0, 0)] * values.ndim
    upper_pad = [(0, 0)] * values.ndim
    lower_pad[along_axis] = (1, 0)
    upper_pad[along_axis] = (0, 1)
    return jnp.pad(values, lower_pad) + jnp.pad(values, upper_pad)


def spread(values, along_axis):
    lower_pad = [(0, 0)] * values.ndim
    upper_pad = [(0, 0)] * values.ndim
    lower_pad[along_axis] = (1, 0)
    upper_pad[along_axis] = (0, 1)
    return jnp.pad(values, lower_pad) - jnp.pad(values, upper_pad)


def operate(values, coeffs):
    depth_faces, row_faces, column_faces = coeffs
    padded = extended(values, (("vox", 0),), 1)
    flux_depth = depth_faces[:, None] * (padded[1:] - padded[:-1])
    result = leakage * values + (flux_depth[:-1] - flux_depth[1:])
    result = result + spread(row_faces[:, None] * (values[:, :, 1:] - values[:, :, :-1]), 2)
    result = result + spread(
        column_faces[:, None] * (values[:, :, :, 1:] - values[:, :, :, :-1]), 3
    )
    return result


def inner(left_factor, right_factor):
    return jnp.sum(left_factor * right_factor, axis=(0, 2, 3))


def widen(vector):
    return vector[None, :, None, None]


def pattern_sum(local_terms):
    return lax.psum(local_terms, "vox")


def solve_pattern(right_side, initial, coeffs, diagonal):
    solution = initial
    residue = right_side - operate(solution, coeffs)
    precond = residue / diagonal
    direction = precond
    current = pattern_sum(inner(residue, precond))
    for iteration in range(ITERS):
        applied = operate(direction, coeffs)
        step_size = current / pattern_sum(inner(direction, applied))
        solution = solution + widen(step_size) * direction
        residue = residue - widen(step_size) * applied
        if iteration + 1 < ITERS:
            precond = residue / diagonal
            following = pattern_sum(inner(residue, precond))
            direction = precond + widen(following / current) * direction
            current = following
    return solution


def per_device_in_place(conductivity, warm_forward, warm_adjoint, electrodes, patterns, observed):
    plane_count, pattern_count, row_count, column_count = warm_forward.shape
    position = lax.axis_index("vox")
    layers = lax.axis_size("vox")
    strength = 2.0 * math.sqrt(layers * plane_count * row_count * column_count)
    data_weight = 0.1 * strength
    lower_open = (position > 0).astype(jnp.float32)
    upper_open = (position < layers - 1).astype(jnp.float32)
    padded_sigma = extended(conductivity, (("vox", 0),), 1)
    face_mask = jnp.concatenate(
        [lower_open[None], jnp.ones((plane_count - 1,), jnp.float32), upper_open[None]]
    )
    depth_faces = 0.5 * (padded_sigma[1:] + padded_sigma[:-1]) * face_mask[:, None, None]
    row_faces = 0.5 * (conductivity[:, 1:] + conductivity[:, :-1])
    column_faces = 0.5 * (conductivity[:, :, 1:] + conductivity[:, :, :-1])
    coeffs = (depth_faces, row_faces, column_faces)
    diagonal = (
        leakage
        + (depth_faces[:-1] + depth_faces[1:])
        + both_sides(row_faces, 1)
        + both_sides(column_faces, 2)
    )
    diagonal = diagonal[:, None]
    electrode_ids = jnp.arange(electrodes.shape[0], dtype=jnp.int32)
    picked = jnp.sum(
        jnp.where(
            patterns[:, :, None] == electrode_ids[None, None, :], electrodes[None, None, :], 0
        ),
        axis=2,
    )
    offset = position * (plane_count * row_count * column_count)
    local_cell = picked - offset
    grid_shape = (plane_count, 1, row_count, column_count)
    cell_index = (
        lax.broadcasted_iota(jnp.int32, grid_shape, 0) * row_count
        + lax.broadcasted_iota(jnp.int32, grid_shape, 2)
    ) * column_count + lax.broadcasted_iota(jnp.int32, grid_shape, 3)

    def marker(which_one):
        return (cell_index == local_cell[:, which_one][None, :, None, None]).astype(jnp.float32)

    forward = solve_pattern(strength * (marker(0) - marker(1)), warm_forward, coeffs, diagonal)
    probe_weights = marker(2) - marker(3)
    predicted = lax.psum(inner(probe_weights, forward), "vox")
    misfit = predicted - observed
    adjoint = solve_pattern(
        widen(data_weight * misfit) * probe_weights, warm_adjoint, coeffs, diagonal
    )
    stacked = jnp.concatenate([forward, adjoint], axis=1)
    padded_pair = extended(stacked, (("vox", 0),), 1)
    padded_forward = padded_pair[:, :pattern_count]
    padded_adjoint = padded_pair[:, pattern_count:]
    depth_products = jnp.sum(
        (padded_forward[1:] - padded_forward[:-1]) * (padded_adjoint[1:] - padded_adjoint[:-1]),
        axis=1,
    )
    depth_products = depth_products * face_mask[:, None, None]
    grad_depth = depth_products[:-1] + depth_products[1:]
    row_products = jnp.sum(
        (forward[:, :, 1:] - forward[:, :, :-1]) * (adjoint[:, :, 1:] - adjoint[:, :, :-1]), axis=1
    )
    column_products = jnp.sum(
        (forward[:, :, :, 1:] - forward[:, :, :, :-1])
        * (adjoint[:, :, :, 1:] - adjoint[:, :, :, :-1]),
        axis=1,
    )
    local_gradient = -0.5 * (
        grad_depth + both_sides(row_products, 1) + both_sides(column_products, 2)
    )
    gradient = lax.psum(local_gradient, "pat")
    return (gradient, predicted)


def per_device(conductivity, warm_forward, *rest):
    size = lax.axis_size("vox")
    groups = lax.axis_size("pat")
    exchange = warm_forward.shape[1] == size and size % CORES == 0
    exchange = exchange and size & (size - 1) == 0 and groups & (groups - 1) == 0
    form = per_device_exchanged if exchange else per_device_in_place
    return form(conductivity, warm_forward, *rest)


def solution(mesh):
    in_specs = (
        P("vox", None, None),
        P("vox", "pat", None, None),
        P("vox", "pat", None, None),
        P(),
        P("pat", None),
        P("pat"),
    )
    out_specs = (P("vox", None, None), P("pat"))
    return jax.shard_map(
        per_device, mesh=mesh, in_specs=in_specs, out_specs=out_specs, check_vma=False
    )
```

```python
import functools
import math

import jax
import jax.numpy as jnp
from jax import lax
from jax.experimental import pallas as pl
from jax.experimental.pallas import tpu as pltpu
from jax.sharding import PartitionSpec as P


ITERS = 2


leakage = 0.05

CORES = 2
SPARE = 8
ROWS = 256


VMEM = pl.BlockSpec(memory_space=pltpu.VMEM)
SMEM = pl.BlockSpec(memory_space=pltpu.SMEM)
HBM = pl.BlockSpec(memory_space=pltpu.HBM)


def call(body, out_shape, operands, in_specs, scratch=(), limit=1):
    moved = sum(4 * a.size for a in operands) + sum(4 * o.size for o in out_shape)
    return pl.pallas_call(
        body,
        out_shape=out_shape,
        in_specs=in_specs,
        out_specs=[VMEM] * len(out_shape),
        scratch_shapes=list(scratch),
        compiler_params=pltpu.CompilerParams(vmem_limit_bytes=limit << 20),
        cost_estimate=pl.CostEstimate(flops=moved, bytes_accessed=moved, transcendentals=0),
    )(*operands)


def shape(*dims):
    return jax.ShapeDtypeStruct(dims, jnp.float32)


def total(acc):
    return jnp.sum(acc, keepdims=True)


def fold(rows):
    return jnp.sum(rows.reshape(rows.shape[0] // 8, 8, rows.shape[1]), axis=0)


def ahead(rows):
    return pltpu.roll(rows, rows.shape[1] - 1, 1)


def behind(rows):
    return pltpu.roll(rows, 1, 1)


def padded(planes, height, width):
    return ((planes + 2) * height, width)


def clear_edges(*refs, height):
    for ref in refs:
        zero = jnp.zeros((height, ref.shape[1]), ref.dtype)
        ref[:height] = zero
        ref[ref.shape[0] - height :] = zero


def each_chunk(rows, height, body, start, size=ROWS):
    size = math.gcd(size, rows)

    def step(index, carry):
        base = pl.multiple_of(height + index * size, math.gcd(size, height))

        def at(ref, offset=0, value=None):
            where = pl.ds(base + offset, size)
            if value is None:
                return ref[where, :]
            ref[where, :] = value

        return body(at, index * size, carry)

    return lax.fori_loop(0, rows // size, step, start)


def neighbours(at, field, depth, rows, columns, height):
    here, column = at(field), at(columns)
    result = at(depth) * at(field, height) + at(depth, -height) * at(field, -height)
    result += at(rows) * at(field, 1)
    result += at(rows, -1) * at(field, -1)
    result += column * ahead(here) + behind(column * here)
    return here, result


def my_place():
    position = lax.axis_index("vox")
    return lax.div(position, CORES), lax.rem(position, CORES), position


def copy_all(pairs, sems):
    copies = [
        pltpu.make_async_copy(source, target, sems.at[number])
        for number, (source, target) in enumerate(pairs)
    ]
    for copy in copies:
        copy.start()
    for copy in copies:
        copy.wait()


def stage_kernel(share, conductivity, forward, fetched, *refs):
    chip = my_place()[0]
    size = fetched.shape[0]
    first = lax.rem(lax.axis_index("pat"), share) * size
    pairs = [(conductivity.at[pl.ds(first, size)], fetched)]
    for step, out in enumerate(refs[:-1]):
        pairs.append((forward.at[:, pl.ds(CORES * (chip ^ step), CORES)], out))
    copy_all(pairs, refs[-1])


def stage_adjoint_kernel(adjoint, own, give, sems):
    core = my_place()[1]
    pairs = []
    for plane in range(own.shape[0]):
        for other in range(own.shape[1]):
            pairs.append((adjoint.at[plane, CORES * other + 1 - core], give.at[plane, other]))
            pairs.append((adjoint.at[plane, CORES * other + core], own.at[plane, other]))
    copy_all(pairs, sems)


def pack_kernel(own, got, *outs):
    place = my_place()
    planes = own.shape[0]
    for step, out in enumerate(outs):
        other = place[0] ^ step
        for plane in range(planes):
            out[0, plane] = own[plane, other]
            out[1, plane] = got[plane, other]


def sort_kernel(*refs):
    place = my_place()
    blocks, keep, give = refs[:-2], refs[-2], refs[-1]
    for step, block in enumerate(blocks):
        for plane in range(block.shape[0]):
            keep[step, plane] = block[plane, place[1]]
            give[step, plane] = block[plane, 1 - place[1]]


def plane_rows(place, step, relative, plane, planes, height):
    level = ((place[0] ^ step) * CORES + (place[1] ^ relative)) * planes + plane
    return pl.ds(pl.multiple_of((level + 1) * height, height), height)


def coefficient_kernel(chips, share, own, others, depth, rows, columns, scale, root, sigma):
    place = my_place()
    total_planes, height, width = own.shape
    planes = total_planes // chips
    count = chips * CORES * planes
    part_planes = planes // share
    mine = lax.rem(lax.axis_index("pat"), share)
    clear_edges(depth, rows, columns, scale, root, sigma, height=height)
    fetched = [(0, plane) for plane in range(planes)]
    for half in range(share):
        owner = lax.rem(mine + half, share)
        for step in range(1, chips):
            fetched += [(step, owner * part_planes + plane) for plane in range(part_planes)]
    for relative, source in enumerate((own, others)):
        for number, (step, plane) in enumerate(fetched):
            sigma[plane_rows(place, step, relative, plane, planes, height), :] = source[number]
    row = lax.broadcasted_iota(jnp.int32, (height, width), 0)
    lane = lax.broadcasted_iota(jnp.int32, (height, width), 1)
    row_ahead, row_behind, lane_ahead = row < height - 1, row > 0, lane < width - 1

    def diagonals(at, first, carry):
        here = at(sigma)
        upper = jnp.where(first // height < count - 1, 0.5, 0.0) * (here + at(sigma, height))
        row_face = jnp.where(row_ahead, 0.5 * (here + at(sigma, 1)), 0.0)
        row_faces = row_face + jnp.where(row_behind, 0.5 * (here + at(sigma, -1)), 0.0)
        face = jnp.where(lane_ahead, 0.5 * (here + ahead(here)), 0.0)
        diagonal = leakage + (at(depth, -height) + upper) + row_faces + (behind(face) + face)
        inverse = lax.rsqrt(diagonal)
        inverse = inverse * (1.5 - 0.5 * diagonal * inverse * inverse)
        at(depth, value=upper)
        at(rows, value=row_face)
        at(columns, value=face)
        at(scale, value=inverse)
        at(root, value=diagonal * inverse)
        return carry

    each_chunk(count * height, height, diagonals, 0, height)

    def couplings(at, first, carry):
        size = at(scale)
        at(depth, value=at(depth) * (size * at(scale, height)))
        at(rows, value=at(rows) * (size * at(scale, 1)))
        at(columns, value=at(columns) * (size * ahead(size)))
        return carry

    each_chunk(count * height, height, couplings, 0)


def spot(ref, cell, height):
    width = ref.shape[1]
    lane = lax.broadcasted_iota(jnp.int32, (1, width), 1)
    return pl.ds(height + cell // width, 1), lane == cell % width


def add_at(ref, scale, cell, value, height):
    row, hit = spot(ref, cell, height)
    ref[row, :] += jnp.where(hit, value * scale[row, :], 0.0)


def value_at(ref, cell, height):
    row, hit = spot(ref, cell, height)
    return total(jnp.where(hit, ref[row, :], 0.0))


def solve_in_place(coefficients, sources, field, residue, applied, later, end, height):
    depth, rows, columns, scale = coefficients
    width = field.shape[1]
    size = field.shape[0] - 2 * height
    nothing = jnp.zeros((8, width), jnp.float32)
    clear_edges(field, residue, applied, height=height)

    def first(at, index, carry):
        here, sums = neighbours(at, field, depth, rows, columns, height)
        at(residue, value=sums - here)
        return carry

    each_chunk(size, height, first, 0)
    for cell, value in sources:
        add_at(residue, scale, cell, value, height)

    def second(at, index, carry):
        squares, products = carry
        here, sums = neighbours(at, residue, depth, rows, columns, height)
        product = here - sums
        at(applied, value=product)
        return squares + fold(here * here), products + fold(here * product)

    squares, products = each_chunk(size, height, second, (nothing, nothing))
    current, energy = total(squares), total(products)
    step_size = current / energy

    def third(at, index, carry):
        squares, products, energies = carry

        def left(offset=0):
            return at(residue, offset) - step_size * at(applied, offset)

        here = left()
        at(later, value=here)
        sums = at(depth, -height) * left(-height) + at(rows, -1) * left(-1)
        sums += behind(at(columns) * here)
        squares = squares + fold(here * here)
        products = products + fold(here * at(applied))
        return squares, products, energies + fold(here * (here - 2.0 * sums))

    squares, products, energies = each_chunk(size, height, third, (nothing,) * 3)
    following, cross, own = total(squares), total(products), total(energies)
    ratio = following / current
    last_size = following / (own + ratio * (2.0 * cross + ratio * energy))
    first_size = step_size + last_size * ratio

    def fifth(at, index, carry):
        moved = at(field) + first_size * at(residue) + last_size * at(later)
        end(at, at(scale) * moved)
        return carry

    each_chunk(size, height, fifth, 0)


def electrode(place, electrodes, patterns, which):
    return electrodes[patterns[which, place[2]]]


def forward_kernel(strength, electrodes, patterns, *refs):
    place = my_place()
    depth, rows, columns, scale, root, own, others = refs[:7]
    *slopes, voltage, field, residue, applied, later, result = refs[7:]
    chips, planes, height, width = own.shape
    for step in range(chips):
        for relative, source in enumerate((own, others)):
            for plane in range(planes):
                where = plane_rows(place, step, relative, plane, planes, height)
                field[where, :] = source[step, plane] * root[where, :]
    plus, minus, high, low = (
        electrode(place, electrodes, patterns, which) for which in range(4)
    )

    def end(at, potential):
        at(result, value=potential)

    solve_in_place(
        (depth, rows, columns, scale),
        ((plus, strength), (minus, -strength)),
        field, residue, applied, later, end, height,
    )
    clear_edges(result, *slopes, height=height)
    count = chips * CORES * planes
    row = lax.broadcasted_iota(jnp.int32, (height, 1), 0)
    lane = lax.broadcasted_iota(jnp.int32, (1, width), 1)
    row_weight = jnp.where(row < height - 1, -0.5, 0.0)
    lane_weight = jnp.where(lane < width - 1, -0.5, 0.0)
    along_depth, along_row, along_column = slopes

    def slope(at, first, carry):
        here = at(result)
        depth_weight = jnp.where(first // height < count - 1, -0.5, 0.0)
        at(along_depth, value=depth_weight * (at(result, height) - here))
        at(along_row, value=row_weight * (at(result, 1) - here))
        at(along_column, value=lane_weight * (ahead(here) - here))
        return carry

    each_chunk(count * height, height, slope, 0, height)
    seen = value_at(result, high, height) - value_at(result, low, height)
    voltage[...] = jnp.broadcast_to(seen, voltage.shape)


def adjoint_kernel(weight, electrodes, patterns, observed, *refs):
    place = my_place()
    depth, rows, columns, scale, root, *slopes, voltage = refs[:9]
    *blocks, adjoint, given, field, residue, applied, later = refs[9:]
    planes, height, _ = blocks[0].shape[1:]
    for step, block in enumerate(blocks):
        for relative in range(CORES):
            for plane in range(planes):
                where = plane_rows(place, step, relative, plane, planes, height)
                field[where, :] = block[relative, plane] * root[where, :]
    weighted = weight * (voltage[0:1, :] - observed[place[2]])
    high = electrode(place, electrodes, patterns, 2)
    low = electrode(place, electrodes, patterns, 3)

    def end(at, potential):
        at(adjoint, value=potential)

    solve_in_place(
        (depth, rows, columns, scale),
        ((high, weighted), (low, -weighted)),
        field, residue, applied, later, end, height,
    )
    clear_edges(adjoint, height=height)
    gradient_blocks(place, 1, slopes, voltage, adjoint, given, planes, height)


def gradient_kernel(planes, height, *refs):
    place = my_place()
    *slopes, voltage, adjoint, kept = refs
    gradient_blocks(place, 0, slopes, voltage, adjoint, kept, planes, height)


def gradient_blocks(place, relative, slopes, voltage, adjoint, out, planes, height):
    along_depth, along_row, along_column = slopes
    chips, width = out.shape[0], out.shape[2]
    size = planes * height

    def step(block, carry):
        start = plane_rows(place, block, relative, 0, planes, height).start

        def at(ref, offset=0):
            return ref[pl.ds(start + offset, size), :]

        here = at(adjoint)
        result = at(along_depth) * (at(adjoint, height) - here)
        result += at(along_depth, -height) * (here - at(adjoint, -height))
        result += at(along_row) * (at(adjoint, 1) - here)
        result += at(along_row, -1) * (here - at(adjoint, -1))
        face = at(along_column) * (ahead(here) - here)
        out[block, :size, :] = result + (face + behind(face))
        return carry

    lax.fori_loop(0, chips, step, 0)
    lane = lax.broadcasted_iota(jnp.int32, (SPARE, width), 1)
    note = jnp.where(lane == place[2], voltage[...], 0.0)
    for block in range(chips):
        out[block, size:, :] = note


def swap(values, axis, size, bit):
    return lax.ppermute(values, axis, [(i, i ^ bit) for i in range(size)])


def per_device_exchanged(
    conductivity, warm_forward, warm_adjoint, electrodes, patterns, observed
):
    plane_count, pattern_count, row_count, column_count = warm_forward.shape
    layers = lax.axis_size("vox")
    groups = lax.axis_size("pat")
    chips = layers // CORES
    strength = 2.0 * math.sqrt(layers * plane_count * row_count * column_count)
    plane = (row_count, column_count)
    whole = shape(*padded(layers * plane_count, *plane))
    room = pltpu.VMEM(whole.shape, jnp.float32)

    def chip_swap(values, step):
        return swap(values, "vox", layers, CORES * step)

    def core_swap(values):
        return swap(values, "vox", layers, 1)

    share = 2 if groups % 2 == 0 and plane_count % 2 == 0 else 1

    def in_place(values):
        return pltpu.with_memory_space_constraint(values, pltpu.HBM)

    fetched, *sends = call(
        functools.partial(stage_kernel, share),
        [shape(plane_count // share, *plane)] + [shape(plane_count, CORES, *plane)] * chips,
        (in_place(conductivity), in_place(warm_forward)),
        [HBM, HBM],
        scratch=[pltpu.SemaphoreType.DMA((1 + chips,))],
    )
    order = list(reversed(range(1, chips)))
    fetched = {step: chip_swap(fetched, step) for step in order}
    fetched = [fetched[step] for step in range(1, chips)]
    blocks = {step: chip_swap(sends[step], step) for step in order}
    blocks = [sends[0]] + [blocks[step] for step in range(1, chips)]
    own, give = call(
        stage_adjoint_kernel,
        [shape(plane_count, chips, *plane)] * 2,
        (in_place(warm_adjoint),),
        [HBM],
        scratch=[pltpu.SemaphoreType.DMA((2 * chips * plane_count,))],
    )
    got = core_swap(give)
    packed = call(
        pack_kernel, [shape(CORES, plane_count, *plane)] * chips, (own, got), [VMEM, VMEM]
    )
    adjoint_blocks = {0: packed[0]}
    for step in order:
        adjoint_blocks[step] = chip_swap(packed[step], step)
    adjoint_blocks = [adjoint_blocks[step] for step in range(chips)]
    others = [swap(jnp.concatenate(fetched), "pat", groups, 1)] if share == 2 else []
    own_sigma = jnp.concatenate([conductivity] + fetched + others)
    other_sigma = core_swap(own_sigma)
    coefficients = call(
        functools.partial(coefficient_kernel, chips, share),
        [whole] * 5,
        (own_sigma, other_sigma),
        [VMEM, VMEM],
        scratch=[room],
        limit=3,
    )
    keep, pass_on = call(
        sort_kernel,
        [shape(chips, plane_count, *plane)] * 2,
        tuple(blocks), [VMEM] * chips,
    )
    received = core_swap(pass_on)
    *slopes, voltage = call(
        functools.partial(forward_kernel, strength),
        [whole] * 3 + [shape(SPARE, column_count)],
        (electrodes, patterns.T, *coefficients, keep, received),
        [SMEM] * 2 + [VMEM] * 7,
        scratch=[room] * 5,
        limit=8,
    )
    block = shape(chips, plane_count * row_count + SPARE, column_count)
    adjoint, given = call(
        functools.partial(adjoint_kernel, 0.1 * strength),
        [whole, block],
        (
            electrodes, patterns.T, observed,
            *coefficients, *slopes, voltage, *adjoint_blocks,
        ),
        [SMEM] * 3 + [VMEM] * (9 + chips),
        scratch=[room] * 4,
        limit=8,
    )
    (kept,) = call(
        functools.partial(gradient_kernel, plane_count, row_count),
        [block],
        (*slopes, voltage, adjoint),
        [VMEM] * 5,
    )
    summed = kept + core_swap(given)
    first_rows = row_count * ((plane_count + 1) // 2)
    cuts = ((0, first_rows), (first_rows, plane_count * row_count + SPARE))
    cut = [summed[:, low:high] for low, high in cuts]
    pieces = [piece[0] for piece in cut]
    received = {}
    for step in range(1, chips):
        for number, piece in enumerate(cut):
            received[number, step] = chip_swap(piece[step], step)
    for number in range(len(pieces)):
        for step in range(1, chips):
            pieces[number] = pieces[number] + received[number, step]
    predicted = pieces[-1][-SPARE, :pattern_count]
    pieces[-1] = pieces[-1][:-SPARE]
    bit = 1
    while bit < groups:
        for number in range(len(pieces)):
            pieces[number] = pieces[number] + swap(pieces[number], "pat", groups, bit)
        bit *= 2
    gradient = jnp.concatenate(pieces).reshape(plane_count, *plane)
    return gradient, predicted


def extended(block, sides, width):
    for axis, dim in sides:
        count = lax.axis_size(axis)
        forward = [(i, i + 1) for i in range(count - 1)]
        backward = [(target, source) for source, target in forward]
        low = lax.ppermute(
            lax.slice_in_dim(block, block.shape[dim] - width, None, axis=dim), axis, forward
        )
        high = lax.ppermute(lax.slice_in_dim(block, 0, width, axis=dim), axis, backward)
        block = jnp.concatenate([low, block, high], axis=dim)
    return block


def both_sides(values, along_axis):
    lower_pad = [(0, 0)] * values.ndim
    upper_pad = [(0, 0)] * values.ndim
    lower_pad[along_axis] = (1, 0)
    upper_pad[along_axis] = (0, 1)
    return jnp.pad(values, lower_pad) + jnp.pad(values, upper_pad)


def spread(values, along_axis):
    lower_pad = [(0, 0)] * values.ndim
    upper_pad = [(0, 0)] * values.ndim
    lower_pad[along_axis] = (1, 0)
    upper_pad[along_axis] = (0, 1)
    return jnp.pad(values, lower_pad) - jnp.pad(values, upper_pad)


def operate(values, coeffs):
    depth_faces, row_faces, column_faces = coeffs
    padded = extended(values, (("vox", 0),), 1)
    flux_depth = depth_faces[:, None] * (padded[1:] - padded[:-1])
    result = leakage * values + (flux_depth[:-1] - flux_depth[1:])
    result = result + spread(row_faces[:, None] * (values[:, :, 1:] - values[:, :, :-1]), 2)
    result = result + spread(
        column_faces[:, None] * (values[:, :, :, 1:] - values[:, :, :, :-1]), 3
    )
    return result


def inner(left_factor, right_factor):
    return jnp.sum(left_factor * right_factor, axis=(0, 2, 3))


def widen(vector):
    return vector[None, :, None, None]


def pattern_sum(local_terms):
    return lax.psum(local_terms, "vox")


def solve_pattern(right_side, initial, coeffs, diagonal):
    solution = initial
    residue = right_side - operate(solution, coeffs)
    precond = residue / diagonal
    direction = precond
    current = pattern_sum(inner(residue, precond))
    for iteration in range(ITERS):
        applied = operate(direction, coeffs)
        step_size = current / pattern_sum(inner(direction, applied))
        solution = solution + widen(step_size) * direction
        residue = residue - widen(step_size) * applied
        if iteration + 1 < ITERS:
            precond = residue / diagonal
            following = pattern_sum(inner(residue, precond))
            direction = precond + widen(following / current) * direction
            current = following
    return solution


def per_device_in_place(conductivity, warm_forward, warm_adjoint, electrodes, patterns, observed):
    plane_count, pattern_count, row_count, column_count = warm_forward.shape
    position = lax.axis_index("vox")
    layers = lax.axis_size("vox")
    strength = 2.0 * math.sqrt(layers * plane_count * row_count * column_count)
    data_weight = 0.1 * strength
    lower_open = (position > 0).astype(jnp.float32)
    upper_open = (position < layers - 1).astype(jnp.float32)
    padded_sigma = extended(conductivity, (("vox", 0),), 1)
    face_mask = jnp.concatenate(
        [lower_open[None], jnp.ones((plane_count - 1,), jnp.float32), upper_open[None]]
    )
    depth_faces = 0.5 * (padded_sigma[1:] + padded_sigma[:-1]) * face_mask[:, None, None]
    row_faces = 0.5 * (conductivity[:, 1:] + conductivity[:, :-1])
    column_faces = 0.5 * (conductivity[:, :, 1:] + conductivity[:, :, :-1])
    coeffs = (depth_faces, row_faces, column_faces)
    diagonal = (
        leakage
        + (depth_faces[:-1] + depth_faces[1:])
        + both_sides(row_faces, 1)
        + both_sides(column_faces, 2)
    )
    diagonal = diagonal[:, None]
    electrode_ids = jnp.arange(electrodes.shape[0], dtype=jnp.int32)
    picked = jnp.sum(
        jnp.where(
            patterns[:, :, None] == electrode_ids[None, None, :], electrodes[None, None, :], 0
        ),
        axis=2,
    )
    offset = position * (plane_count * row_count * column_count)
    local_cell = picked - offset
    grid_shape = (plane_count, 1, row_count, column_count)
    cell_index = (
        lax.broadcasted_iota(jnp.int32, grid_shape, 0) * row_count
        + lax.broadcasted_iota(jnp.int32, grid_shape, 2)
    ) * column_count + lax.broadcasted_iota(jnp.int32, grid_shape, 3)

    def marker(which_one):
        return (cell_index == local_cell[:, which_one][None, :, None, None]).astype(jnp.float32)

    forward = solve_pattern(strength * (marker(0) - marker(1)), warm_forward, coeffs, diagonal)
    probe_weights = marker(2) - marker(3)
    predicted = lax.psum(inner(probe_weights, forward), "vox")
    misfit = predicted - observed
    adjoint = solve_pattern(
        widen(data_weight * misfit) * probe_weights, warm_adjoint, coeffs, diagonal
    )
    stacked = jnp.concatenate([forward, adjoint], axis=1)
    padded_pair = extended(stacked, (("vox", 0),), 1)
    padded_forward = padded_pair[:, :pattern_count]
    padded_adjoint = padded_pair[:, pattern_count:]
    depth_products = jnp.sum(
        (padded_forward[1:] - padded_forward[:-1]) * (padded_adjoint[1:] - padded_adjoint[:-1]),
        axis=1,
    )
    depth_products = depth_products * face_mask[:, None, None]
    grad_depth = depth_products[:-1] + depth_products[1:]
    row_products = jnp.sum(
        (forward[:, :, 1:] - forward[:, :, :-1]) * (adjoint[:, :, 1:] - adjoint[:, :, :-1]), axis=1
    )
    column_products = jnp.sum(
        (forward[:, :, :, 1:] - forward[:, :, :, :-1])
        * (adjoint[:, :, :, 1:] - adjoint[:, :, :, :-1]),
        axis=1,
    )
    local_gradient = -0.5 * (
        grad_depth + both_sides(row_products, 1) + both_sides(column_products, 2)
    )
    gradient = lax.psum(local_gradient, "pat")
    return (gradient, predicted)


def per_device(conductivity, warm_forward, *rest):
    size = lax.axis_size("vox")
    groups = lax.axis_size("pat")
    exchange = warm_forward.shape[1] == size and size % CORES == 0
    exchange = exchange and size & (size - 1) == 0 and groups & (groups - 1) == 0
    form = per_device_exchanged if exchange else per_device_in_place
    return form(conductivity, warm_forward, *rest)


def solution(mesh):
    in_specs = (
        P("vox", None, None),
        P("vox", "pat", None, None),
        P("vox", "pat", None, None),
        P(),
        P("pat", None),
        P("pat"),
    )
    out_specs = (P("vox", None, None), P("pat"))
    return jax.shard_map(
        per_device, mesh=mesh, in_specs=in_specs, out_specs=out_specs, check_vma=False
    )
```

```python
import functools
import math

import jax
import jax.numpy as jnp
from jax import lax
from jax.experimental import pallas as pl
from jax.experimental.pallas import tpu as pltpu
from jax.sharding import PartitionSpec as P


ITERS = 2


leakage = 0.05

CORES = 2
SPARE = 8
ROWS = 256


VMEM = pl.BlockSpec(memory_space=pltpu.VMEM)
SMEM = pl.BlockSpec(memory_space=pltpu.SMEM)
HBM = pl.BlockSpec(memory_space=pltpu.HBM)


def call(body, out_shape, operands, in_specs, scratch=(), limit=1):
    moved = sum(4 * a.size for a in operands) + sum(4 * o.size for o in out_shape)
    return pl.pallas_call(
        body,
        out_shape=out_shape,
        in_specs=in_specs,
        out_specs=[VMEM] * len(out_shape),
        scratch_shapes=list(scratch),
        compiler_params=pltpu.CompilerParams(vmem_limit_bytes=limit << 20),
        cost_estimate=pl.CostEstimate(flops=moved, bytes_accessed=moved, transcendentals=0),
    )(*operands)


def shape(*dims):
    return jax.ShapeDtypeStruct(dims, jnp.float32)


def total(acc):
    return jnp.sum(acc, keepdims=True)


def fold(rows):
    return jnp.sum(rows.reshape(rows.shape[0] // 8, 8, rows.shape[1]), axis=0)


def ahead(rows):
    return pltpu.roll(rows, rows.shape[1] - 1, 1)


def behind(rows):
    return pltpu.roll(rows, 1, 1)


def padded(planes, height, width):
    return ((planes + 2) * height, width)


def clear_edges(*refs, height):
    for ref in refs:
        zero = jnp.zeros((height, ref.shape[1]), ref.dtype)
        ref[:height] = zero
        ref[ref.shape[0] - height :] = zero


def each_chunk(rows, height, body, start, size=ROWS):
    size = math.gcd(size, rows)

    def step(index, carry):
        base = pl.multiple_of(height + index * size, math.gcd(size, height))

        def at(ref, offset=0, value=None):
            where = pl.ds(base + offset, size)
            if value is None:
                return ref[where, :]
            ref[where, :] = value

        return body(at, index * size, carry)

    return lax.fori_loop(0, rows // size, step, start)


def neighbours(at, field, depth, rows, columns, height):
    here, column = at(field), at(columns)
    result = at(depth) * at(field, height) + at(depth, -height) * at(field, -height)
    result += at(rows) * at(field, 1)
    result += at(rows, -1) * at(field, -1)
    result += column * ahead(here) + behind(column * here)
    return here, result


def my_place():
    position = lax.axis_index("vox")
    return lax.div(position, CORES), lax.rem(position, CORES), position


def copy_all(pairs, sems):
    copies = [
        pltpu.make_async_copy(source, target, sems.at[number])
        for number, (source, target) in enumerate(pairs)
    ]
    for copy in copies:
        copy.start()
    for copy in copies:
        copy.wait()


def stage_kernel(share, conductivity, forward, fetched, *refs):
    chip = my_place()[0]
    size = fetched.shape[0]
    first = lax.rem(lax.axis_index("pat"), share) * size
    pairs = [(conductivity.at[pl.ds(first, size)], fetched)]
    for step, out in enumerate(refs[:-1]):
        pairs.append((forward.at[:, pl.ds(CORES * (chip ^ step), CORES)], out))
    copy_all(pairs, refs[-1])


def stage_adjoint_kernel(adjoint, own, give, sems):
    core = my_place()[1]
    pairs = []
    for plane in range(own.shape[0]):
        for other in range(own.shape[1]):
            pairs.append((adjoint.at[plane, CORES * other + 1 - core], give.at[plane, other]))
            pairs.append((adjoint.at[plane, CORES * other + core], own.at[plane, other]))
    copy_all(pairs, sems)


def pack_kernel(own, got, *outs):
    place = my_place()
    planes = own.shape[0]
    for step, out in enumerate(outs):
        other = place[0] ^ step
        for plane in range(planes):
            out[0, plane] = own[plane, other]
            out[1, plane] = got[plane, other]


def sort_kernel(*refs):
    place = my_place()
    blocks, keep, give = refs[:-2], refs[-2], refs[-1]
    for step, block in enumerate(blocks):
        for plane in range(block.shape[0]):
            keep[step, plane] = block[plane, place[1]]
            give[step, plane] = block[plane, 1 - place[1]]


def plane_rows(place, step, relative, plane, planes, height):
    level = ((place[0] ^ step) * CORES + (place[1] ^ relative)) * planes + plane
    return pl.ds(pl.multiple_of((level + 1) * height, height), height)


def coefficient_kernel(chips, share, own, others, depth, rows, columns, scale, root, sigma):
    place = my_place()
    total_planes, height, width = own.shape
    planes = total_planes // chips
    count = chips * CORES * planes
    part_planes = planes // share
    mine = lax.rem(lax.axis_index("pat"), share)
    clear_edges(depth, rows, columns, scale, root, sigma, height=height)
    fetched = [(0, plane) for plane in range(planes)]
    for half in range(share):
        owner = lax.rem(mine + half, share)
        for step in range(1, chips):
            fetched += [(step, owner * part_planes + plane) for plane in range(part_planes)]
    for relative, source in enumerate((own, others)):
        for number, (step, plane) in enumerate(fetched):
            sigma[plane_rows(place, step, relative, plane, planes, height), :] = source[number]
    row = lax.broadcasted_iota(jnp.int32, (height, width), 0)
    lane = lax.broadcasted_iota(jnp.int32, (height, width), 1)
    row_ahead, row_behind, lane_ahead = row < height - 1, row > 0, lane < width - 1

    def diagonals(at, first, carry):
        here = at(sigma)
        upper = jnp.where(first // height < count - 1, 0.5, 0.0) * (here + at(sigma, height))
        row_face = jnp.where(row_ahead, 0.5 * (here + at(sigma, 1)), 0.0)
        row_faces = row_face + jnp.where(row_behind, 0.5 * (here + at(sigma, -1)), 0.0)
        face = jnp.where(lane_ahead, 0.5 * (here + ahead(here)), 0.0)
        diagonal = leakage + (at(depth, -height) + upper) + row_faces + (behind(face) + face)
        inverse = lax.rsqrt(diagonal)
        inverse = inverse * (1.5 - 0.5 * diagonal * inverse * inverse)
        at(depth, value=upper)
        at(rows, value=row_face)
        at(columns, value=face)
        at(scale, value=inverse)
        at(root, value=diagonal * inverse)
        return carry

    each_chunk(count * height, height, diagonals, 0, height)

    def couplings(at, first, carry):
        size = at(scale)
        at(depth, value=at(depth) * (size * at(scale, height)))
        at(rows, value=at(rows) * (size * at(scale, 1)))
        at(columns, value=at(columns) * (size * ahead(size)))
        return carry

    each_chunk(count * height, height, couplings, 0)


def spot(ref, cell, height):
    width = ref.shape[1]
    lane = lax.broadcasted_iota(jnp.int32, (1, width), 1)
    return pl.ds(height + cell // width, 1), lane == cell % width


def add_at(ref, scale, cell, value, height):
    row, hit = spot(ref, cell, height)
    ref[row, :] += jnp.where(hit, value * scale[row, :], 0.0)


def value_at(ref, cell, height):
    row, hit = spot(ref, cell, height)
    return total(jnp.where(hit, ref[row, :], 0.0))


def solve_in_place(coefficients, sources, field, residue, applied, later, end, height):
    depth, rows, columns, scale = coefficients
    width = field.shape[1]
    size = field.shape[0] - 2 * height
    nothing = jnp.zeros((8, width), jnp.float32)
    clear_edges(field, residue, applied, height=height)

    def first(at, index, carry):
        here, sums = neighbours(at, field, depth, rows, columns, height)
        at(residue, value=sums - here)
        return carry

    each_chunk(size, height, first, 0)
    for cell, value in sources:
        add_at(residue, scale, cell, value, height)

    def second(at, index, carry):
        squares, products = carry
        here, sums = neighbours(at, residue, depth, rows, columns, height)
        product = here - sums
        at(applied, value=product)
        return squares + fold(here * here), products + fold(here * product)

    squares, products = each_chunk(size, height, second, (nothing, nothing))
    current, energy = total(squares), total(products)
    step_size = current / energy

    def third(at, index, carry):
        squares, products, energies = carry

        def left(offset=0):
            return at(residue, offset) - step_size * at(applied, offset)

        here = left()
        at(later, value=here)
        sums = at(depth, -height) * left(-height) + at(rows, -1) * left(-1)
        sums += behind(at(columns) * here)
        squares = squares + fold(here * here)
        products = products + fold(here * at(applied))
        return squares, products, energies + fold(here * (here - 2.0 * sums))

    squares, products, energies = each_chunk(size, height, third, (nothing,) * 3)
    following, cross, own = total(squares), total(products), total(energies)
    ratio = following / current
    last_size = following / (own + ratio * (2.0 * cross + ratio * energy))
    first_size = step_size + last_size * ratio

    def fifth(at, index, carry):
        moved = at(field) + first_size * at(residue) + last_size * at(later)
        end(at, at(scale) * moved)
        return carry

    each_chunk(size, height, fifth, 0)


def electrode(place, electrodes, patterns, which):
    return electrodes[patterns[which, place[2]]]


def forward_kernel(strength, electrodes, patterns, *refs):
    place = my_place()
    depth, rows, columns, scale, root, own, others = refs[:7]
    *slopes, voltage, field, residue, applied, later, result = refs[7:]
    chips, planes, height, width = own.shape
    for step in range(chips):
        for relative, source in enumerate((own, others)):
            for plane in range(planes):
                where = plane_rows(place, step, relative, plane, planes, height)
                field[where, :] = source[step, plane] * root[where, :]
    plus, minus, high, low = (
        electrode(place, electrodes, patterns, which) for which in range(4)
    )

    def end(at, potential):
        at(result, value=potential)

    solve_in_place(
        (depth, rows, columns, scale),
        ((plus, strength), (minus, -strength)),
        field, residue, applied, later, end, height,
    )
    clear_edges(result, *slopes, height=height)
    count = chips * CORES * planes
    row = lax.broadcasted_iota(jnp.int32, (height, 1), 0)
    lane = lax.broadcasted_iota(jnp.int32, (1, width), 1)
    row_weight = jnp.where(row < height - 1, -0.5, 0.0)
    lane_weight = jnp.where(lane < width - 1, -0.5, 0.0)
    along_depth, along_row, along_column = slopes

    def slope(at, first, carry):
        here = at(result)
        depth_weight = jnp.where(first // height < count - 1, -0.5, 0.0)
        at(along_depth, value=depth_weight * (at(result, height) - here))
        at(along_row, value=row_weight * (at(result, 1) - here))
        at(along_column, value=lane_weight * (ahead(here) - here))
        return carry

    each_chunk(count * height, height, slope, 0, height)
    seen = value_at(result, high, height) - value_at(result, low, height)
    voltage[...] = jnp.broadcast_to(seen, voltage.shape)


def adjoint_kernel(weight, electrodes, patterns, observed, *refs):
    place = my_place()
    depth, rows, columns, scale, root, *slopes, voltage = refs[:9]
    *blocks, adjoint, given, field, residue, applied, later = refs[9:]
    planes, height, _ = blocks[0].shape[1:]
    for step, block in enumerate(blocks):
        for relative in range(CORES):
            for plane in range(planes):
                where = plane_rows(place, step, relative, plane, planes, height)
                field[where, :] = block[relative, plane] * root[where, :]
    weighted = weight * (voltage[0:1, :] - observed[place[2]])
    high = electrode(place, electrodes, patterns, 2)
    low = electrode(place, electrodes, patterns, 3)

    def end(at, potential):
        at(adjoint, value=potential)

    solve_in_place(
        (depth, rows, columns, scale),
        ((high, weighted), (low, -weighted)),
        field, residue, applied, later, end, height,
    )
    clear_edges(adjoint, height=height)
    gradient_blocks(place, 1, slopes, voltage, adjoint, given, planes, height)


def gradient_kernel(planes, height, *refs):
    place = my_place()
    *slopes, voltage, adjoint, kept = refs
    gradient_blocks(place, 0, slopes, voltage, adjoint, kept, planes, height)


def gradient_blocks(place, relative, slopes, voltage, adjoint, out, planes, height):
    along_depth, along_row, along_column = slopes
    chips, width = out.shape[0], out.shape[2]
    size = planes * height

    def step(block, carry):
        start = plane_rows(place, block, relative, 0, planes, height).start

        def at(ref, offset=0):
            return ref[pl.ds(start + offset, size), :]

        here = at(adjoint)
        result = at(along_depth) * (at(adjoint, height) - here)
        result += at(along_depth, -height) * (here - at(adjoint, -height))
        result += at(along_row) * (at(adjoint, 1) - here)
        result += at(along_row, -1) * (here - at(adjoint, -1))
        face = at(along_column) * (ahead(here) - here)
        out[block, :size, :] = result + (face + behind(face))
        return carry

    lax.fori_loop(0, chips, step, 0)
    lane = lax.broadcasted_iota(jnp.int32, (SPARE, width), 1)
    note = jnp.where(lane == place[2], voltage[...], 0.0)
    for block in range(chips):
        out[block, size:, :] = note


def swap(values, axis, size, bit):
    return lax.ppermute(values, axis, [(i, i ^ bit) for i in range(size)])


def per_device_exchanged(
    conductivity, warm_forward, warm_adjoint, electrodes, patterns, observed
):
    plane_count, pattern_count, row_count, column_count = warm_forward.shape
    layers = lax.axis_size("vox")
    groups = lax.axis_size("pat")
    chips = layers // CORES
    strength = 2.0 * math.sqrt(layers * plane_count * row_count * column_count)
    plane = (row_count, column_count)
    whole = shape(*padded(layers * plane_count, *plane))
    room = pltpu.VMEM(whole.shape, jnp.float32)

    def chip_swap(values, step):
        return swap(values, "vox", layers, CORES * step)

    def core_swap(values):
        return swap(values, "vox", layers, 1)

    share = 2 if groups % 2 == 0 and plane_count % 2 == 0 else 1

    def in_place(values):
        return pltpu.with_memory_space_constraint(values, pltpu.HBM)

    fetched, *sends = call(
        functools.partial(stage_kernel, share),
        [shape(plane_count // share, *plane)] + [shape(plane_count, CORES, *plane)] * chips,
        (in_place(conductivity), in_place(warm_forward)),
        [HBM, HBM],
        scratch=[pltpu.SemaphoreType.DMA((1 + chips,))],
    )
    sigma_got, blocks, adjoint_blocks = {}, {0: sends[0]}, {}
    for step in range(1, chips):
        sigma_got[step] = chip_swap(fetched, step)
        blocks[step] = chip_swap(sends[step], step)
    fetched = [sigma_got[step] for step in range(1, chips)]
    blocks = [blocks[step] for step in range(chips)]
    own, give = call(
        stage_adjoint_kernel,
        [shape(plane_count, chips, *plane)] * 2,
        (in_place(warm_adjoint),),
        [HBM],
        scratch=[pltpu.SemaphoreType.DMA((2 * chips * plane_count,))],
    )
    got = core_swap(give)
    packed = call(
        pack_kernel, [shape(CORES, plane_count, *plane)] * chips, (own, got), [VMEM, VMEM]
    )
    adjoint_blocks[0] = packed[0]
    for step in range(1, chips):
        adjoint_blocks[step] = chip_swap(packed[step], step)
    adjoint_blocks = [adjoint_blocks[step] for step in range(chips)]
    others = [swap(jnp.concatenate(fetched), "pat", groups, 1)] if share == 2 else []
    own_sigma = jnp.concatenate([conductivity] + fetched + others)
    other_sigma = core_swap(own_sigma)
    coefficients = call(
        functools.partial(coefficient_kernel, chips, share),
        [whole] * 5,
        (own_sigma, other_sigma),
        [VMEM, VMEM],
        scratch=[room],
        limit=3,
    )
    keep, pass_on = call(
        sort_kernel, [shape(chips, plane_count, *plane)] * 2, tuple(blocks), [VMEM] * chips
    )
    received = core_swap(pass_on)
    *slopes, voltage = call(
        functools.partial(forward_kernel, strength),
        [whole] * 3 + [shape(SPARE, column_count)],
        (electrodes, patterns.T, *coefficients, keep, received),
        [SMEM] * 2 + [VMEM] * 7,
        scratch=[room] * 5,
        limit=8,
    )
    block = shape(chips, plane_count * row_count + SPARE, column_count)
    adjoint, given = call(
        functools.partial(adjoint_kernel, 0.1 * strength),
        [whole, block],
        (
            electrodes, patterns.T, observed,
            *coefficients, *slopes, voltage, *adjoint_blocks,
        ),
        [SMEM] * 3 + [VMEM] * (9 + chips),
        scratch=[room] * 4,
        limit=8,
    )
    (kept,) = call(
        functools.partial(gradient_kernel, plane_count, row_count),
        [block],
        (*slopes, voltage, adjoint),
        [VMEM] * 5,
    )
    summed = kept + core_swap(given)
    first_rows = row_count * ((plane_count + 1) // 2)
    cuts = ((0, first_rows), (first_rows, plane_count * row_count + SPARE))
    cut = [summed[:, low:high] for low, high in cuts]
    pieces = [piece[0] for piece in cut]
    received = {}
    for step in range(1, chips):
        for number, piece in enumerate(cut):
            received[number, step] = chip_swap(piece[step], step)
    for number in range(len(pieces)):
        for step in range(1, chips):
            pieces[number] = pieces[number] + received[number, step]
    predicted = pieces[-1][-SPARE, :pattern_count]
    pieces[-1] = pieces[-1][:-SPARE]
    bit = 1
    while bit < groups:
        for number in range(len(pieces)):
            pieces[number] = pieces[number] + swap(pieces[number], "pat", groups, bit)
        bit *= 2
    gradient = jnp.concatenate(pieces).reshape(plane_count, *plane)
    return gradient, predicted


def extended(block, sides, width):
    for axis, dim in sides:
        count = lax.axis_size(axis)
        forward = [(i, i + 1) for i in range(count - 1)]
        backward = [(target, source) for source, target in forward]
        low = lax.ppermute(
            lax.slice_in_dim(block, block.shape[dim] - width, None, axis=dim), axis, forward
        )
        high = lax.ppermute(lax.slice_in_dim(block, 0, width, axis=dim), axis, backward)
        block = jnp.concatenate([low, block, high], axis=dim)
    return block


def both_sides(values, along_axis):
    lower_pad = [(0, 0)] * values.ndim
    upper_pad = [(0, 0)] * values.ndim
    lower_pad[along_axis] = (1, 0)
    upper_pad[along_axis] = (0, 1)
    return jnp.pad(values, lower_pad) + jnp.pad(values, upper_pad)


def spread(values, along_axis):
    lower_pad = [(0, 0)] * values.ndim
    upper_pad = [(0, 0)] * values.ndim
    lower_pad[along_axis] = (1, 0)
    upper_pad[along_axis] = (0, 1)
    return jnp.pad(values, lower_pad) - jnp.pad(values, upper_pad)


def operate(values, coeffs):
    depth_faces, row_faces, column_faces = coeffs
    padded = extended(values, (("vox", 0),), 1)
    flux_depth = depth_faces[:, None] * (padded[1:] - padded[:-1])
    result = leakage * values + (flux_depth[:-1] - flux_depth[1:])
    result = result + spread(row_faces[:, None] * (values[:, :, 1:] - values[:, :, :-1]), 2)
    result = result + spread(
        column_faces[:, None] * (values[:, :, :, 1:] - values[:, :, :, :-1]), 3
    )
    return result


def inner(left_factor, right_factor):
    return jnp.sum(left_factor * right_factor, axis=(0, 2, 3))


def widen(vector):
    return vector[None, :, None, None]


def pattern_sum(local_terms):
    return lax.psum(local_terms, "vox")


def solve_pattern(right_side, initial, coeffs, diagonal):
    solution = initial
    residue = right_side - operate(solution, coeffs)
    precond = residue / diagonal
    direction = precond
    current = pattern_sum(inner(residue, precond))
    for iteration in range(ITERS):
        applied = operate(direction, coeffs)
        step_size = current / pattern_sum(inner(direction, applied))
        solution = solution + widen(step_size) * direction
        residue = residue - widen(step_size) * applied
        if iteration + 1 < ITERS:
            precond = residue / diagonal
            following = pattern_sum(inner(residue, precond))
            direction = precond + widen(following / current) * direction
            current = following
    return solution


def per_device_in_place(conductivity, warm_forward, warm_adjoint, electrodes, patterns, observed):
    plane_count, pattern_count, row_count, column_count = warm_forward.shape
    position = lax.axis_index("vox")
    layers = lax.axis_size("vox")
    strength = 2.0 * math.sqrt(layers * plane_count * row_count * column_count)
    data_weight = 0.1 * strength
    lower_open = (position > 0).astype(jnp.float32)
    upper_open = (position < layers - 1).astype(jnp.float32)
    padded_sigma = extended(conductivity, (("vox", 0),), 1)
    face_mask = jnp.concatenate(
        [lower_open[None], jnp.ones((plane_count - 1,), jnp.float32), upper_open[None]]
    )
    depth_faces = 0.5 * (padded_sigma[1:] + padded_sigma[:-1]) * face_mask[:, None, None]
    row_faces = 0.5 * (conductivity[:, 1:] + conductivity[:, :-1])
    column_faces = 0.5 * (conductivity[:, :, 1:] + conductivity[:, :, :-1])
    coeffs = (depth_faces, row_faces, column_faces)
    diagonal = (
        leakage
        + (depth_faces[:-1] + depth_faces[1:])
        + both_sides(row_faces, 1)
        + both_sides(column_faces, 2)
    )
    diagonal = diagonal[:, None]
    electrode_ids = jnp.arange(electrodes.shape[0], dtype=jnp.int32)
    picked = jnp.sum(
        jnp.where(
            patterns[:, :, None] == electrode_ids[None, None, :], electrodes[None, None, :], 0
        ),
        axis=2,
    )
    offset = position * (plane_count * row_count * column_count)
    local_cell = picked - offset
    grid_shape = (plane_count, 1, row_count, column_count)
    cell_index = (
        lax.broadcasted_iota(jnp.int32, grid_shape, 0) * row_count
        + lax.broadcasted_iota(jnp.int32, grid_shape, 2)
    ) * column_count + lax.broadcasted_iota(jnp.int32, grid_shape, 3)

    def marker(which_one):
        return (cell_index == local_cell[:, which_one][None, :, None, None]).astype(jnp.float32)

    forward = solve_pattern(strength * (marker(0) - marker(1)), warm_forward, coeffs, diagonal)
    probe_weights = marker(2) - marker(3)
    predicted = lax.psum(inner(probe_weights, forward), "vox")
    misfit = predicted - observed
    adjoint = solve_pattern(
        widen(data_weight * misfit) * probe_weights, warm_adjoint, coeffs, diagonal
    )
    stacked = jnp.concatenate([forward, adjoint], axis=1)
    padded_pair = extended(stacked, (("vox", 0),), 1)
    padded_forward = padded_pair[:, :pattern_count]
    padded_adjoint = padded_pair[:, pattern_count:]
    depth_products = jnp.sum(
        (padded_forward[1:] - padded_forward[:-1]) * (padded_adjoint[1:] - padded_adjoint[:-1]),
        axis=1,
    )
    depth_products = depth_products * face_mask[:, None, None]
    grad_depth = depth_products[:-1] + depth_products[1:]
    row_products = jnp.sum(
        (forward[:, :, 1:] - forward[:, :, :-1]) * (adjoint[:, :, 1:] - adjoint[:, :, :-1]), axis=1
    )
    column_products = jnp.sum(
        (forward[:, :, :, 1:] - forward[:, :, :, :-1])
        * (adjoint[:, :, :, 1:] - adjoint[:, :, :, :-1]),
        axis=1,
    )
    local_gradient = -0.5 * (
        grad_depth + both_sides(row_products, 1) + both_sides(column_products, 2)
    )
    gradient = lax.psum(local_gradient, "pat")
    return (gradient, predicted)


def per_device(conductivity, warm_forward, *rest):
    size = lax.axis_size("vox")
    groups = lax.axis_size("pat")
    exchange = warm_forward.shape[1] == size and size % CORES == 0
    exchange = exchange and size & (size - 1) == 0 and groups & (groups - 1) == 0
    form = per_device_exchanged if exchange else per_device_in_place
    return form(conductivity, warm_forward, *rest)


def solution(mesh):
    in_specs = (
        P("vox", None, None),
        P("vox", "pat", None, None),
        P("vox", "pat", None, None),
        P(),
        P("pat", None),
        P("pat"),
    )
    out_specs = (P("vox", None, None), P("pat"))
    return jax.shard_map(
        per_device, mesh=mesh, in_specs=in_specs, out_specs=out_specs, check_vma=False
    )
```

```python
import functools
import math

import jax
import jax.numpy as jnp
from jax import lax
from jax.experimental import pallas as pl
from jax.experimental.pallas import tpu as pltpu
from jax.sharding import PartitionSpec as P


ITERS = 2


leakage = 0.05

CORES = 2
SPARE = 8
ROWS = 256


VMEM = pl.BlockSpec(memory_space=pltpu.VMEM)
SMEM = pl.BlockSpec(memory_space=pltpu.SMEM)
HBM = pl.BlockSpec(memory_space=pltpu.HBM)


def call(body, out_shape, operands, in_specs, scratch=(), limit=1):
    moved = sum(4 * a.size for a in operands) + sum(4 * o.size for o in out_shape)
    return pl.pallas_call(
        body,
        out_shape=out_shape,
        in_specs=in_specs,
        out_specs=[VMEM] * len(out_shape),
        scratch_shapes=list(scratch),
        compiler_params=pltpu.CompilerParams(vmem_limit_bytes=limit << 20),
        cost_estimate=pl.CostEstimate(flops=moved, bytes_accessed=moved, transcendentals=0),
    )(*operands)


def shape(*dims):
    return jax.ShapeDtypeStruct(dims, jnp.float32)


def total(acc):
    return jnp.sum(acc, keepdims=True)


def fold(rows):
    return jnp.sum(rows.reshape(rows.shape[0] // 8, 8, rows.shape[1]), axis=0)


def ahead(rows):
    return pltpu.roll(rows, rows.shape[1] - 1, 1)


def behind(rows):
    return pltpu.roll(rows, 1, 1)


def padded(planes, height, width):
    return ((planes + 2) * height, width)


def clear_edges(*refs, height):
    for ref in refs:
        zero = jnp.zeros((height, ref.shape[1]), ref.dtype)
        ref[:height] = zero
        ref[ref.shape[0] - height :] = zero


def each_chunk(rows, height, body, start, size=ROWS):
    size = math.gcd(size, rows)

    def step(index, carry):
        base = pl.multiple_of(height + index * size, math.gcd(size, height))

        def at(ref, offset=0, value=None):
            where = pl.ds(base + offset, size)
            if value is None:
                return ref[where, :]
            ref[where, :] = value

        return body(at, index * size, carry)

    return lax.fori_loop(0, rows // size, step, start)


def neighbours(at, field, depth, rows, columns, height):
    here, column = at(field), at(columns)
    result = at(depth) * at(field, height) + at(depth, -height) * at(field, -height)
    result += at(rows) * at(field, 1)
    result += at(rows, -1) * at(field, -1)
    result += column * ahead(here) + behind(column * here)
    return here, result


def my_place():
    position = lax.axis_index("vox")
    return lax.div(position, CORES), lax.rem(position, CORES), position


def copy_all(pairs, sems):
    copies = [
        pltpu.make_async_copy(source, target, sems.at[number])
        for number, (source, target) in enumerate(pairs)
    ]
    for copy in copies:
        copy.start()
    for copy in copies:
        copy.wait()


def stage_kernel(share, conductivity, forward, fetched, *refs):
    chip = my_place()[0]
    size = fetched.shape[0]
    first = lax.rem(lax.axis_index("pat"), share) * size
    pairs = [(conductivity.at[pl.ds(first, size)], fetched)]
    for step, out in enumerate(refs[:-1]):
        pairs.append((forward.at[:, pl.ds(CORES * (chip ^ step), CORES)], out))
    copy_all(pairs, refs[-1])


def stage_adjoint_kernel(adjoint, own, give, sems):
    core = my_place()[1]
    pairs = []
    for plane in range(own.shape[0]):
        for other in range(own.shape[1]):
            pairs.append((adjoint.at[plane, CORES * other + 1 - core], give.at[plane, other]))
            pairs.append((adjoint.at[plane, CORES * other + core], own.at[plane, other]))
    copy_all(pairs, sems)


def pack_kernel(own, got, *outs):
    place = my_place()
    planes = own.shape[0]
    for step, out in enumerate(outs):
        other = place[0] ^ step
        for plane in range(planes):
            out[0, plane] = own[plane, other]
            out[1, plane] = got[plane, other]


def sort_kernel(*refs):
    place = my_place()
    blocks, keep, give = refs[:-2], refs[-2], refs[-1]
    for step, block in enumerate(blocks):
        for plane in range(block.shape[0]):
            keep[step, plane] = block[plane, place[1]]
            give[step, plane] = block[plane, 1 - place[1]]


def plane_rows(place, step, relative, plane, planes, height):
    level = ((place[0] ^ step) * CORES + (place[1] ^ relative)) * planes + plane
    return pl.ds(pl.multiple_of((level + 1) * height, height), height)


def coefficient_kernel(chips, share, own, others, depth, rows, columns, scale, root, sigma):
    place = my_place()
    total_planes, height, width = own.shape
    planes = total_planes // chips
    count = chips * CORES * planes
    part_planes = planes // share
    mine = lax.rem(lax.axis_index("pat"), share)
    clear_edges(depth, rows, columns, scale, root, sigma, height=height)
    fetched = [(0, plane) for plane in range(planes)]
    for half in range(share):
        owner = lax.rem(mine + half, share)
        for step in range(1, chips):
            fetched += [(step, owner * part_planes + plane) for plane in range(part_planes)]
    for relative, source in enumerate((own, others)):
        for number, (step, plane) in enumerate(fetched):
            sigma[plane_rows(place, step, relative, plane, planes, height), :] = source[number]
    row = lax.broadcasted_iota(jnp.int32, (height, width), 0)
    lane = lax.broadcasted_iota(jnp.int32, (height, width), 1)
    row_ahead, row_behind, lane_ahead = row < height - 1, row > 0, lane < width - 1

    def diagonals(at, first, carry):
        here = at(sigma)
        upper = jnp.where(first // height < count - 1, 0.5, 0.0) * (here + at(sigma, height))
        row_face = jnp.where(row_ahead, 0.5 * (here + at(sigma, 1)), 0.0)
        row_faces = row_face + jnp.where(row_behind, 0.5 * (here + at(sigma, -1)), 0.0)
        face = jnp.where(lane_ahead, 0.5 * (here + ahead(here)), 0.0)
        diagonal = leakage + (at(depth, -height) + upper) + row_faces + (behind(face) + face)
        inverse = lax.rsqrt(diagonal)
        inverse = inverse * (1.5 - 0.5 * diagonal * inverse * inverse)
        at(depth, value=upper)
        at(rows, value=row_face)
        at(columns, value=face)
        at(scale, value=inverse)
        at(root, value=diagonal * inverse)
        return carry

    each_chunk(count * height, height, diagonals, 0, height)

    def couplings(at, first, carry):
        size = at(scale)
        at(depth, value=at(depth) * (size * at(scale, height)))
        at(rows, value=at(rows) * (size * at(scale, 1)))
        at(columns, value=at(columns) * (size * ahead(size)))
        return carry

    each_chunk(count * height, height, couplings, 0)


def spot(ref, cell, height):
    width = ref.shape[1]
    lane = lax.broadcasted_iota(jnp.int32, (1, width), 1)
    return pl.ds(height + cell // width, 1), lane == cell % width


def add_at(ref, scale, cell, value, height):
    row, hit = spot(ref, cell, height)
    ref[row, :] += jnp.where(hit, value * scale[row, :], 0.0)


def value_at(ref, cell, height):
    row, hit = spot(ref, cell, height)
    return total(jnp.where(hit, ref[row, :], 0.0))


def solve_in_place(coefficients, sources, field, residue, applied, later, end, height):
    depth, rows, columns, scale = coefficients
    width = field.shape[1]
    size = field.shape[0] - 2 * height
    nothing = jnp.zeros((8, width), jnp.float32)
    clear_edges(field, residue, applied, height=height)

    def first(at, index, carry):
        here, sums = neighbours(at, field, depth, rows, columns, height)
        at(residue, value=sums - here)
        return carry

    each_chunk(size, height, first, 0)
    for cell, value in sources:
        add_at(residue, scale, cell, value, height)

    def second(at, index, carry):
        squares, products = carry
        here, sums = neighbours(at, residue, depth, rows, columns, height)
        product = here - sums
        at(applied, value=product)
        return squares + fold(here * here), products + fold(here * product)

    squares, products = each_chunk(size, height, second, (nothing, nothing))
    current, energy = total(squares), total(products)
    step_size = current / energy

    def third(at, index, carry):
        squares, products, energies = carry

        def left(offset=0):
            return at(residue, offset) - step_size * at(applied, offset)

        here = left()
        at(later, value=here)
        sums = at(depth, -height) * left(-height) + at(rows, -1) * left(-1)
        sums += behind(at(columns) * here)
        squares = squares + fold(here * here)
        products = products + fold(here * at(applied))
        return squares, products, energies + fold(here * (here - 2.0 * sums))

    squares, products, energies = each_chunk(size, height, third, (nothing,) * 3)
    following, cross, own = total(squares), total(products), total(energies)
    ratio = following / current
    last_size = following / (own + ratio * (2.0 * cross + ratio * energy))
    first_size = step_size + last_size * ratio

    def fifth(at, index, carry):
        moved = at(field) + first_size * at(residue) + last_size * at(later)
        end(at, at(scale) * moved)
        return carry

    each_chunk(size, height, fifth, 0)


def electrode(place, electrodes, patterns, which):
    return electrodes[patterns[which, place[2]]]


def forward_kernel(strength, electrodes, patterns, *refs):
    place = my_place()
    depth, rows, columns, scale, root, own, others = refs[:7]
    *slopes, voltage, field, residue, applied, later, result = refs[7:]
    chips, planes, height, width = own.shape
    for step in range(chips):
        for relative, source in enumerate((own, others)):
            for plane in range(planes):
                where = plane_rows(place, step, relative, plane, planes, height)
                field[where, :] = source[step, plane] * root[where, :]
    plus, minus, high, low = (
        electrode(place, electrodes, patterns, which) for which in range(4)
    )

    def end(at, potential):
        at(result, value=potential)

    solve_in_place(
        (depth, rows, columns, scale),
        ((plus, strength), (minus, -strength)),
        field, residue, applied, later, end, height,
    )
    clear_edges(result, *slopes, height=height)
    count = chips * CORES * planes
    row = lax.broadcasted_iota(jnp.int32, (height, 1), 0)
    lane = lax.broadcasted_iota(jnp.int32, (1, width), 1)
    row_weight = jnp.where(row < height - 1, -0.5, 0.0)
    lane_weight = jnp.where(lane < width - 1, -0.5, 0.0)
    along_depth, along_row, along_column = slopes

    def slope(at, first, carry):
        here = at(result)
        depth_weight = jnp.where(first // height < count - 1, -0.5, 0.0)
        at(along_depth, value=depth_weight * (at(result, height) - here))
        at(along_row, value=row_weight * (at(result, 1) - here))
        at(along_column, value=lane_weight * (ahead(here) - here))
        return carry

    each_chunk(count * height, height, slope, 0, height)
    seen = value_at(result, high, height) - value_at(result, low, height)
    voltage[...] = jnp.broadcast_to(seen, voltage.shape)


def adjoint_kernel(weight, electrodes, patterns, observed, *refs):
    place = my_place()
    depth, rows, columns, scale, root, *slopes, voltage = refs[:9]
    *blocks, adjoint, given, last_given, field, residue, applied, later = refs[9:]
    planes, height, _ = blocks[0].shape[1:]
    for step, block in enumerate(blocks):
        for relative in range(CORES):
            for plane in range(planes):
                where = plane_rows(place, step, relative, plane, planes, height)
                field[where, :] = block[relative, plane] * root[where, :]
    weighted = weight * (voltage[0:1, :] - observed[place[2]])
    high = electrode(place, electrodes, patterns, 2)
    low = electrode(place, electrodes, patterns, 3)

    def end(at, potential):
        at(adjoint, value=potential)

    solve_in_place(
        (depth, rows, columns, scale),
        ((high, weighted), (low, -weighted)),
        field, residue, applied, later, end, height,
    )
    clear_edges(adjoint, height=height)
    gradient_pieces(place, 1, slopes, voltage, adjoint, (given, last_given), planes, height)


def gradient_kernel(planes, height, *refs):
    *slopes, voltage, adjoint, kept, last_kept = refs
    gradient_pieces(
        my_place(), 0, slopes, voltage, adjoint, (kept, last_kept), planes, height
    )


def gradient_pieces(place, relative, slopes, voltage, adjoint, outs, planes, height):
    along_depth, along_row, along_column = slopes
    chips, rows, width = outs[0].shape
    size = planes * height

    def step(block, carry):
        start = plane_rows(place, block, relative, 0, planes, height).start

        def at(ref, offset=0):
            return ref[pl.ds(start + offset, size), :]

        here = at(adjoint)
        result = at(along_depth) * (at(adjoint, height) - here)
        result += at(along_depth, -height) * (here - at(adjoint, -height))
        result += at(along_row) * (at(adjoint, 1) - here)
        result += at(along_row, -1) * (here - at(adjoint, -1))
        face = at(along_column) * (ahead(here) - here)
        result += face + behind(face)
        outs[0][block] = result[:rows]
        outs[1][block, : size - rows, :] = result[rows:]
        return carry

    lax.fori_loop(0, chips, step, 0)
    lane = lax.broadcasted_iota(jnp.int32, (SPARE, width), 1)
    note = jnp.where(lane == place[2], voltage[...], 0.0)
    for block in range(chips):
        outs[1][block, size - rows :, :] = note


def swap(values, axis, size, bit):
    return lax.ppermute(values, axis, [(i, i ^ bit) for i in range(size)])


def per_device_exchanged(
    conductivity, warm_forward, warm_adjoint, electrodes, patterns, observed
):
    plane_count, pattern_count, row_count, column_count = warm_forward.shape
    layers = lax.axis_size("vox")
    groups = lax.axis_size("pat")
    chips = layers // CORES
    strength = 2.0 * math.sqrt(layers * plane_count * row_count * column_count)
    plane = (row_count, column_count)
    whole = shape(*padded(layers * plane_count, *plane))
    room = pltpu.VMEM(whole.shape, jnp.float32)

    def chip_swap(values, step):
        return swap(values, "vox", layers, CORES * step)

    def core_swap(values):
        return swap(values, "vox", layers, 1)

    share = 2 if groups % 2 == 0 and plane_count % 2 == 0 else 1

    def in_place(values):
        return pltpu.with_memory_space_constraint(values, pltpu.HBM)

    fetched, *sends = call(
        functools.partial(stage_kernel, share),
        [shape(plane_count // share, *plane)] + [shape(plane_count, CORES, *plane)] * chips,
        (in_place(conductivity), in_place(warm_forward)),
        [HBM, HBM],
        scratch=[pltpu.SemaphoreType.DMA((1 + chips,))],
    )
    sigma_got, blocks, adjoint_blocks = {}, {0: sends[0]}, {}
    for step in range(1, chips):
        sigma_got[step] = chip_swap(fetched, step)
        blocks[step] = chip_swap(sends[step], step)
    fetched = [sigma_got[step] for step in range(1, chips)]
    blocks = [blocks[step] for step in range(chips)]
    own, give = call(
        stage_adjoint_kernel,
        [shape(plane_count, chips, *plane)] * 2,
        (in_place(warm_adjoint),),
        [HBM],
        scratch=[pltpu.SemaphoreType.DMA((2 * chips * plane_count,))],
    )
    got = core_swap(give)
    packed = call(
        pack_kernel, [shape(CORES, plane_count, *plane)] * chips, (own, got), [VMEM, VMEM]
    )
    adjoint_blocks[0] = packed[0]
    for step in range(1, chips):
        adjoint_blocks[step] = chip_swap(packed[step], step)
    adjoint_blocks = [adjoint_blocks[step] for step in range(chips)]
    others = [swap(jnp.concatenate(fetched), "pat", groups, 1)] if share == 2 else []
    own_sigma = jnp.concatenate([conductivity] + fetched + others)
    other_sigma = core_swap(own_sigma)
    coefficients = call(
        functools.partial(coefficient_kernel, chips, share),
        [whole] * 5,
        (own_sigma, other_sigma),
        [VMEM, VMEM],
        scratch=[room],
        limit=3,
    )
    keep, pass_on = call(
        sort_kernel, [shape(chips, plane_count, *plane)] * 2, tuple(blocks), [VMEM] * chips
    )
    received = core_swap(pass_on)
    *slopes, voltage = call(
        functools.partial(forward_kernel, strength),
        [whole] * 3 + [shape(SPARE, column_count)],
        (electrodes, patterns.T, *coefficients, keep, received),
        [SMEM] * 2 + [VMEM] * 7,
        scratch=[room] * 5,
        limit=8,
    )
    cut = (plane_count + 1) // 2 * row_count
    sizes = (cut, plane_count * row_count - cut + SPARE)
    pair = [shape(chips, size, column_count) for size in sizes]
    adjoint, *given = call(
        functools.partial(adjoint_kernel, 0.1 * strength),
        [whole] + pair,
        (
            electrodes, patterns.T, observed,
            *coefficients, *slopes, voltage, *adjoint_blocks,
        ),
        [SMEM] * 3 + [VMEM] * (9 + chips),
        scratch=[room] * 4,
        limit=8,
    )
    received = []
    for piece in given:
        received.append(core_swap(piece))
    kept = call(
        functools.partial(gradient_kernel, plane_count, row_count),
        pair,
        (*slopes, voltage, adjoint),
        [VMEM] * 5,
    )
    summed, pieces = [], []
    for number in range(len(pair)):
        summed.append(kept[number] + received[number])
    for piece in summed:
        got = []
        for step in range(1, chips):
            got.append(chip_swap(piece[step], step))
        pieces.append(piece[0] + sum(got[1:], got[0]))
    predicted = pieces[-1][-SPARE, :pattern_count]
    pieces[-1] = pieces[-1][:-SPARE]
    bit = 1
    while bit < groups:
        for number in range(len(pieces)):
            pieces[number] = pieces[number] + swap(pieces[number], "pat", groups, bit)
        bit *= 2
    gradient = jnp.concatenate(pieces).reshape(plane_count, *plane)
    return gradient, predicted


def extended(block, sides, width):
    for axis, dim in sides:
        count = lax.axis_size(axis)
        forward = [(i, i + 1) for i in range(count - 1)]
        backward = [(target, source) for source, target in forward]
        low = lax.ppermute(
            lax.slice_in_dim(block, block.shape[dim] - width, None, axis=dim), axis, forward
        )
        high = lax.ppermute(lax.slice_in_dim(block, 0, width, axis=dim), axis, backward)
        block = jnp.concatenate([low, block, high], axis=dim)
    return block


def both_sides(values, along_axis):
    lower_pad = [(0, 0)] * values.ndim
    upper_pad = [(0, 0)] * values.ndim
    lower_pad[along_axis] = (1, 0)
    upper_pad[along_axis] = (0, 1)
    return jnp.pad(values, lower_pad) + jnp.pad(values, upper_pad)


def spread(values, along_axis):
    lower_pad = [(0, 0)] * values.ndim
    upper_pad = [(0, 0)] * values.ndim
    lower_pad[along_axis] = (1, 0)
    upper_pad[along_axis] = (0, 1)
    return jnp.pad(values, lower_pad) - jnp.pad(values, upper_pad)


def operate(values, coeffs):
    depth_faces, row_faces, column_faces = coeffs
    padded = extended(values, (("vox", 0),), 1)
    flux_depth = depth_faces[:, None] * (padded[1:] - padded[:-1])
    result = leakage * values + (flux_depth[:-1] - flux_depth[1:])
    result = result + spread(row_faces[:, None] * (values[:, :, 1:] - values[:, :, :-1]), 2)
    result = result + spread(
        column_faces[:, None] * (values[:, :, :, 1:] - values[:, :, :, :-1]), 3
    )
    return result


def inner(left_factor, right_factor):
    return jnp.sum(left_factor * right_factor, axis=(0, 2, 3))


def widen(vector):
    return vector[None, :, None, None]


def pattern_sum(local_terms):
    return lax.psum(local_terms, "vox")


def solve_pattern(right_side, initial, coeffs, diagonal):
    solution = initial
    residue = right_side - operate(solution, coeffs)
    precond = residue / diagonal
    direction = precond
    current = pattern_sum(inner(residue, precond))
    for iteration in range(ITERS):
        applied = operate(direction, coeffs)
        step_size = current / pattern_sum(inner(direction, applied))
        solution = solution + widen(step_size) * direction
        residue = residue - widen(step_size) * applied
        if iteration + 1 < ITERS:
            precond = residue / diagonal
            following = pattern_sum(inner(residue, precond))
            direction = precond + widen(following / current) * direction
            current = following
    return solution


def per_device_in_place(conductivity, warm_forward, warm_adjoint, electrodes, patterns, observed):
    plane_count, pattern_count, row_count, column_count = warm_forward.shape
    position = lax.axis_index("vox")
    layers = lax.axis_size("vox")
    strength = 2.0 * math.sqrt(layers * plane_count * row_count * column_count)
    data_weight = 0.1 * strength
    lower_open = (position > 0).astype(jnp.float32)
    upper_open = (position < layers - 1).astype(jnp.float32)
    padded_sigma = extended(conductivity, (("vox", 0),), 1)
    face_mask = jnp.concatenate(
        [lower_open[None], jnp.ones((plane_count - 1,), jnp.float32), upper_open[None]]
    )
    depth_faces = 0.5 * (padded_sigma[1:] + padded_sigma[:-1]) * face_mask[:, None, None]
    row_faces = 0.5 * (conductivity[:, 1:] + conductivity[:, :-1])
    column_faces = 0.5 * (conductivity[:, :, 1:] + conductivity[:, :, :-1])
    coeffs = (depth_faces, row_faces, column_faces)
    diagonal = (
        leakage
        + (depth_faces[:-1] + depth_faces[1:])
        + both_sides(row_faces, 1)
        + both_sides(column_faces, 2)
    )
    diagonal = diagonal[:, None]
    electrode_ids = jnp.arange(electrodes.shape[0], dtype=jnp.int32)
    picked = jnp.sum(
        jnp.where(
            patterns[:, :, None] == electrode_ids[None, None, :], electrodes[None, None, :], 0
        ),
        axis=2,
    )
    offset = position * (plane_count * row_count * column_count)
    local_cell = picked - offset
    grid_shape = (plane_count, 1, row_count, column_count)
    cell_index = (
        lax.broadcasted_iota(jnp.int32, grid_shape, 0) * row_count
        + lax.broadcasted_iota(jnp.int32, grid_shape, 2)
    ) * column_count + lax.broadcasted_iota(jnp.int32, grid_shape, 3)

    def marker(which_one):
        return (cell_index == local_cell[:, which_one][None, :, None, None]).astype(jnp.float32)

    forward = solve_pattern(strength * (marker(0) - marker(1)), warm_forward, coeffs, diagonal)
    probe_weights = marker(2) - marker(3)
    predicted = lax.psum(inner(probe_weights, forward), "vox")
    misfit = predicted - observed
    adjoint = solve_pattern(
        widen(data_weight * misfit) * probe_weights, warm_adjoint, coeffs, diagonal
    )
    stacked = jnp.concatenate([forward, adjoint], axis=1)
    padded_pair = extended(stacked, (("vox", 0),), 1)
    padded_forward = padded_pair[:, :pattern_count]
    padded_adjoint = padded_pair[:, pattern_count:]
    depth_products = jnp.sum(
        (padded_forward[1:] - padded_forward[:-1]) * (padded_adjoint[1:] - padded_adjoint[:-1]),
        axis=1,
    )
    depth_products = depth_products * face_mask[:, None, None]
    grad_depth = depth_products[:-1] + depth_products[1:]
    row_products = jnp.sum(
        (forward[:, :, 1:] - forward[:, :, :-1]) * (adjoint[:, :, 1:] - adjoint[:, :, :-1]), axis=1
    )
    column_products = jnp.sum(
        (forward[:, :, :, 1:] - forward[:, :, :, :-1])
        * (adjoint[:, :, :, 1:] - adjoint[:, :, :, :-1]),
        axis=1,
    )
    local_gradient = -0.5 * (
        grad_depth + both_sides(row_products, 1) + both_sides(column_products, 2)
    )
    gradient = lax.psum(local_gradient, "pat")
    return (gradient, predicted)


def per_device(conductivity, warm_forward, *rest):
    size = lax.axis_size("vox")
    groups = lax.axis_size("pat")
    exchange = warm_forward.shape[1] == size and size % CORES == 0
    exchange = exchange and size & (size - 1) == 0 and groups & (groups - 1) == 0
    form = per_device_exchanged if exchange else per_device_in_place
    return form(conductivity, warm_forward, *rest)


def solution(mesh):
    in_specs = (
        P("vox", None, None),
        P("vox", "pat", None, None),
        P("vox", "pat", None, None),
        P(),
        P("pat", None),
        P("pat"),
    )
    out_specs = (P("vox", None, None), P("pat"))
    return jax.shard_map(
        per_device, mesh=mesh, in_specs=in_specs, out_specs=out_specs, check_vma=False
    )
```

```python
import functools
import math

import jax
import jax.numpy as jnp
from jax import lax
from jax.experimental import pallas as pl
from jax.experimental.pallas import tpu as pltpu
from jax.sharding import PartitionSpec as P


ITERS = 2


leakage = 0.05

CORES = 2
SPARE = 8
ROWS = 256


VMEM = pl.BlockSpec(memory_space=pltpu.VMEM)
SMEM = pl.BlockSpec(memory_space=pltpu.SMEM)
HBM = pl.BlockSpec(memory_space=pltpu.HBM)


def call(body, out_shape, operands, in_specs, scratch=(), limit=1):
    moved = sum(4 * a.size for a in operands) + sum(4 * o.size for o in out_shape)
    return pl.pallas_call(
        body,
        out_shape=out_shape,
        in_specs=in_specs,
        out_specs=[VMEM] * len(out_shape),
        scratch_shapes=list(scratch),
        compiler_params=pltpu.CompilerParams(vmem_limit_bytes=limit << 20),
        cost_estimate=pl.CostEstimate(flops=moved, bytes_accessed=moved, transcendentals=0),
    )(*operands)


def shape(*dims):
    return jax.ShapeDtypeStruct(dims, jnp.float32)


def total(acc):
    return jnp.sum(acc, keepdims=True)


def fold(rows):
    return jnp.sum(rows.reshape(rows.shape[0] // 8, 8, rows.shape[1]), axis=0)


def ahead(rows):
    return pltpu.roll(rows, rows.shape[1] - 1, 1)


def behind(rows):
    return pltpu.roll(rows, 1, 1)


def padded(planes, height, width):
    return ((planes + 2) * height, width)


def clear_edges(*refs, height):
    for ref in refs:
        zero = jnp.zeros((height, ref.shape[1]), ref.dtype)
        ref[:height] = zero
        ref[ref.shape[0] - height :] = zero


def each_chunk(rows, height, body, start, size=ROWS):
    size = math.gcd(size, rows)

    def step(index, carry):
        base = pl.multiple_of(height + index * size, math.gcd(size, height))

        def at(ref, offset=0, value=None):
            where = pl.ds(base + offset, size)
            if value is None:
                return ref[where, :]
            ref[where, :] = value

        return body(at, index * size, carry)

    return lax.fori_loop(0, rows // size, step, start)


def neighbours(at, field, depth, rows, columns, height):
    here, column = at(field), at(columns)
    result = at(depth) * at(field, height) + at(depth, -height) * at(field, -height)
    result += at(rows) * at(field, 1)
    result += at(rows, -1) * at(field, -1)
    result += column * ahead(here) + behind(column * here)
    return here, result


def my_place():
    position = lax.axis_index("vox")
    return lax.div(position, CORES), lax.rem(position, CORES), position


def copy_all(pairs, sems):
    copies = [
        pltpu.make_async_copy(source, target, sems.at[number])
        for number, (source, target) in enumerate(pairs)
    ]
    for copy in copies:
        copy.start()
    for copy in copies:
        copy.wait()


def stage_kernel(share, conductivity, forward, fetched, *refs):
    chip = my_place()[0]
    size = fetched.shape[0]
    first = lax.rem(lax.axis_index("pat"), share) * size
    pairs = [(conductivity.at[pl.ds(first, size)], fetched)]
    for step, out in enumerate(refs[:-1], start=1):
        pairs.append((forward.at[:, pl.ds(CORES * (chip ^ step), CORES)], out))
    copy_all(pairs, refs[-1])


def stage_rest_kernel(forward, adjoint, kept, own, give, sems):
    chip, core, _ = my_place()
    pairs = [(forward.at[:, pl.ds(CORES * chip, CORES)], kept)]
    for plane in range(own.shape[0]):
        for other in range(own.shape[1]):
            pairs.append((adjoint.at[plane, CORES * other + 1 - core], give.at[plane, other]))
            pairs.append((adjoint.at[plane, CORES * other + core], own.at[plane, other]))
    copy_all(pairs, sems)


def pack_kernel(own, got, *outs):
    place = my_place()
    planes = own.shape[0]
    for step, out in enumerate(outs):
        other = place[0] ^ step
        for plane in range(planes):
            out[0, plane] = own[plane, other]
            out[1, plane] = got[plane, other]


def sort_kernel(*refs):
    place = my_place()
    blocks, keep, give = refs[:-2], refs[-2], refs[-1]
    for step, block in enumerate(blocks):
        for plane in range(block.shape[0]):
            keep[step, plane] = block[plane, place[1]]
            give[step, plane] = block[plane, 1 - place[1]]


def plane_rows(place, step, relative, plane, planes, height):
    level = ((place[0] ^ step) * CORES + (place[1] ^ relative)) * planes + plane
    return pl.ds(pl.multiple_of((level + 1) * height, height), height)


def coefficient_kernel(chips, share, own, others, depth, rows, columns, scale, root, sigma):
    place = my_place()
    total_planes, height, width = own.shape
    planes = total_planes // chips
    count = chips * CORES * planes
    part_planes = planes // share
    mine = lax.rem(lax.axis_index("pat"), share)
    clear_edges(depth, rows, columns, scale, root, sigma, height=height)
    fetched = [(0, plane) for plane in range(planes)]
    for half in range(share):
        owner = lax.rem(mine + half, share)
        for step in range(1, chips):
            fetched += [(step, owner * part_planes + plane) for plane in range(part_planes)]
    for relative, source in enumerate((own, others)):
        for number, (step, plane) in enumerate(fetched):
            sigma[plane_rows(place, step, relative, plane, planes, height), :] = source[number]
    row = lax.broadcasted_iota(jnp.int32, (height, width), 0)
    lane = lax.broadcasted_iota(jnp.int32, (height, width), 1)
    row_ahead, row_behind, lane_ahead = row < height - 1, row > 0, lane < width - 1

    def diagonals(at, first, carry):
        here = at(sigma)
        upper = jnp.where(first // height < count - 1, 0.5, 0.0) * (here + at(sigma, height))
        row_face = jnp.where(row_ahead, 0.5 * (here + at(sigma, 1)), 0.0)
        row_faces = row_face + jnp.where(row_behind, 0.5 * (here + at(sigma, -1)), 0.0)
        face = jnp.where(lane_ahead, 0.5 * (here + ahead(here)), 0.0)
        diagonal = leakage + (at(depth, -height) + upper) + row_faces + (behind(face) + face)
        inverse = lax.rsqrt(diagonal)
        inverse = inverse * (1.5 - 0.5 * diagonal * inverse * inverse)
        at(depth, value=upper)
        at(rows, value=row_face)
        at(columns, value=face)
        at(scale, value=inverse)
        at(root, value=diagonal * inverse)
        return carry

    each_chunk(count * height, height, diagonals, 0, height)

    def couplings(at, first, carry):
        size = at(scale)
        at(depth, value=at(depth) * (size * at(scale, height)))
        at(rows, value=at(rows) * (size * at(scale, 1)))
        at(columns, value=at(columns) * (size * ahead(size)))
        return carry

    each_chunk(count * height, height, couplings, 0)


def spot(ref, cell, height):
    width = ref.shape[1]
    lane = lax.broadcasted_iota(jnp.int32, (1, width), 1)
    return pl.ds(height + cell // width, 1), lane == cell % width


def add_at(ref, scale, cell, value, height):
    row, hit = spot(ref, cell, height)
    ref[row, :] += jnp.where(hit, value * scale[row, :], 0.0)


def value_at(ref, cell, height):
    row, hit = spot(ref, cell, height)
    return total(jnp.where(hit, ref[row, :], 0.0))


def solve_in_place(coefficients, sources, field, residue, applied, later, end, height):
    depth, rows, columns, scale = coefficients
    width = field.shape[1]
    size = field.shape[0] - 2 * height
    nothing = jnp.zeros((8, width), jnp.float32)
    clear_edges(field, residue, applied, height=height)

    def first(at, index, carry):
        here, sums = neighbours(at, field, depth, rows, columns, height)
        at(residue, value=sums - here)
        return carry

    each_chunk(size, height, first, 0)
    for cell, value in sources:
        add_at(residue, scale, cell, value, height)

    def second(at, index, carry):
        squares, products = carry
        here, sums = neighbours(at, residue, depth, rows, columns, height)
        product = here - sums
        at(applied, value=product)
        return squares + fold(here * here), products + fold(here * product)

    squares, products = each_chunk(size, height, second, (nothing, nothing))
    current, energy = total(squares), total(products)
    step_size = current / energy

    def third(at, index, carry):
        squares, products, energies = carry

        def left(offset=0):
            return at(residue, offset) - step_size * at(applied, offset)

        here = left()
        at(later, value=here)
        sums = at(depth, -height) * left(-height) + at(rows, -1) * left(-1)
        sums += behind(at(columns) * here)
        squares = squares + fold(here * here)
        products = products + fold(here * at(applied))
        return squares, products, energies + fold(here * (here - 2.0 * sums))

    squares, products, energies = each_chunk(size, height, third, (nothing,) * 3)
    following, cross, own = total(squares), total(products), total(energies)
    ratio = following / current
    last_size = following / (own + ratio * (2.0 * cross + ratio * energy))
    first_size = step_size + last_size * ratio

    def fifth(at, index, carry):
        moved = at(field) + first_size * at(residue) + last_size * at(later)
        end(at, at(scale) * moved)
        return carry

    each_chunk(size, height, fifth, 0)


def electrode(place, electrodes, patterns, which):
    return electrodes[patterns[which, place[2]]]


def forward_kernel(strength, electrodes, patterns, *refs):
    place = my_place()
    depth, rows, columns, scale, root, own, others = refs[:7]
    *slopes, voltage, field, residue, applied, later, result = refs[7:]
    chips, planes, height, width = own.shape
    for step in range(chips):
        for relative, source in enumerate((own, others)):
            for plane in range(planes):
                where = plane_rows(place, step, relative, plane, planes, height)
                field[where, :] = source[step, plane] * root[where, :]
    plus, minus, high, low = (
        electrode(place, electrodes, patterns, which) for which in range(4)
    )

    def end(at, potential):
        at(result, value=potential)

    solve_in_place(
        (depth, rows, columns, scale),
        ((plus, strength), (minus, -strength)),
        field, residue, applied, later, end, height,
    )
    clear_edges(result, *slopes, height=height)
    count = chips * CORES * planes
    row = lax.broadcasted_iota(jnp.int32, (height, 1), 0)
    lane = lax.broadcasted_iota(jnp.int32, (1, width), 1)
    row_weight = jnp.where(row < height - 1, -0.5, 0.0)
    lane_weight = jnp.where(lane < width - 1, -0.5, 0.0)
    along_depth, along_row, along_column = slopes

    def slope(at, first, carry):
        here = at(result)
        depth_weight = jnp.where(first // height < count - 1, -0.5, 0.0)
        at(along_depth, value=depth_weight * (at(result, height) - here))
        at(along_row, value=row_weight * (at(result, 1) - here))
        at(along_column, value=lane_weight * (ahead(here) - here))
        return carry

    each_chunk(count * height, height, slope, 0, height)
    seen = value_at(result, high, height) - value_at(result, low, height)
    voltage[...] = jnp.broadcast_to(seen, voltage.shape)


def adjoint_kernel(weight, electrodes, patterns, observed, *refs):
    place = my_place()
    depth, rows, columns, scale, root, *slopes, voltage = refs[:9]
    *blocks, adjoint, given, last_given, field, residue, applied, later = refs[9:]
    planes, height, _ = blocks[0].shape[1:]
    for step, block in enumerate(blocks):
        for relative in range(CORES):
            for plane in range(planes):
                where = plane_rows(place, step, relative, plane, planes, height)
                field[where, :] = block[relative, plane] * root[where, :]
    weighted = weight * (voltage[0:1, :] - observed[place[2]])
    high = electrode(place, electrodes, patterns, 2)
    low = electrode(place, electrodes, patterns, 3)

    def end(at, potential):
        at(adjoint, value=potential)

    solve_in_place(
        (depth, rows, columns, scale),
        ((high, weighted), (low, -weighted)),
        field, residue, applied, later, end, height,
    )
    clear_edges(adjoint, height=height)
    gradient_pieces(place, 1, slopes, voltage, adjoint, (given, last_given), planes, height)


def gradient_kernel(planes, height, *refs):
    *slopes, voltage, adjoint, kept, last_kept = refs
    gradient_pieces(
        my_place(), 0, slopes, voltage, adjoint, (kept, last_kept), planes, height
    )


def gradient_pieces(place, relative, slopes, voltage, adjoint, outs, planes, height):
    along_depth, along_row, along_column = slopes
    chips, rows, width = outs[0].shape
    size = planes * height

    def step(block, carry):
        start = plane_rows(place, block, relative, 0, planes, height).start

        def at(ref, offset=0):
            return ref[pl.ds(start + offset, size), :]

        here = at(adjoint)
        result = at(along_depth) * (at(adjoint, height) - here)
        result += at(along_depth, -height) * (here - at(adjoint, -height))
        result += at(along_row) * (at(adjoint, 1) - here)
        result += at(along_row, -1) * (here - at(adjoint, -1))
        face = at(along_column) * (ahead(here) - here)
        result += face + behind(face)
        outs[0][block] = result[:rows]
        outs[1][block, : size - rows, :] = result[rows:]
        return carry

    lax.fori_loop(0, chips, step, 0)
    lane = lax.broadcasted_iota(jnp.int32, (SPARE, width), 1)
    note = jnp.where(lane == place[2], voltage[...], 0.0)
    for block in range(chips):
        outs[1][block, size - rows :, :] = note


def swap(values, axis, size, bit):
    return lax.ppermute(values, axis, [(i, i ^ bit) for i in range(size)])


def per_device_exchanged(
    conductivity, warm_forward, warm_adjoint, electrodes, patterns, observed
):
    plane_count, pattern_count, row_count, column_count = warm_forward.shape
    layers = lax.axis_size("vox")
    groups = lax.axis_size("pat")
    chips = layers // CORES
    strength = 2.0 * math.sqrt(layers * plane_count * row_count * column_count)
    plane = (row_count, column_count)
    whole = shape(*padded(layers * plane_count, *plane))
    room = pltpu.VMEM(whole.shape, jnp.float32)

    def chip_swap(values, step):
        return swap(values, "vox", layers, CORES * step)

    def core_swap(values):
        return swap(values, "vox", layers, 1)

    share = 2 if groups % 2 == 0 and plane_count % 2 == 0 else 1

    def in_place(values):
        return pltpu.with_memory_space_constraint(values, pltpu.HBM)

    fetched, *sends = call(
        functools.partial(stage_kernel, share),
        [shape(plane_count // share, *plane)]
        + [shape(plane_count, CORES, *plane)] * (chips - 1),
        (in_place(conductivity), in_place(warm_forward)),
        [HBM, HBM],
        scratch=[pltpu.SemaphoreType.DMA((chips,))],
    )
    sigma_got, blocks, adjoint_blocks = {}, {}, {}
    for step in range(1, chips):
        sigma_got[step] = chip_swap(fetched, step)
        blocks[step] = chip_swap(sends[step - 1], step)
    fetched = [sigma_got[step] for step in range(1, chips)]
    blocks[0], own, give = call(
        stage_rest_kernel,
        [shape(plane_count, CORES, *plane)] + [shape(plane_count, chips, *plane)] * 2,
        (in_place(warm_forward), in_place(warm_adjoint)),
        [HBM, HBM],
        scratch=[pltpu.SemaphoreType.DMA((1 + 2 * chips * plane_count,))],
    )
    blocks = [blocks[step] for step in range(chips)]
    got = core_swap(give)
    packed = call(
        pack_kernel, [shape(CORES, plane_count, *plane)] * chips, (own, got), [VMEM, VMEM]
    )
    adjoint_blocks[0] = packed[0]
    for step in range(1, chips):
        adjoint_blocks[step] = chip_swap(packed[step], step)
    adjoint_blocks = [adjoint_blocks[step] for step in range(chips)]
    others = [swap(jnp.concatenate(fetched), "pat", groups, 1)] if share == 2 else []
    own_sigma = jnp.concatenate([conductivity] + fetched + others)
    other_sigma = core_swap(own_sigma)
    coefficients = call(
        functools.partial(coefficient_kernel, chips, share),
        [whole] * 5,
        (own_sigma, other_sigma),
        [VMEM, VMEM],
        scratch=[room],
        limit=3,
    )
    keep, pass_on = call(
        sort_kernel, [shape(chips, plane_count, *plane)] * 2, tuple(blocks), [VMEM] * chips
    )
    received = core_swap(pass_on)
    *slopes, voltage = call(
        functools.partial(forward_kernel, strength),
        [whole] * 3 + [shape(SPARE, column_count)],
        (electrodes, patterns.T, *coefficients, keep, received),
        [SMEM] * 2 + [VMEM] * 7,
        scratch=[room] * 5,
        limit=8,
    )
    cut = (plane_count + 1) // 2 * row_count
    sizes = (cut, plane_count * row_count - cut + SPARE)
    pair = [shape(chips, size, column_count) for size in sizes]
    adjoint, *given = call(
        functools.partial(adjoint_kernel, 0.1 * strength),
        [whole] + pair,
        (
            electrodes, patterns.T, observed,
            *coefficients, *slopes, voltage, *adjoint_blocks,
        ),
        [SMEM] * 3 + [VMEM] * (9 + chips),
        scratch=[room] * 4,
        limit=8,
    )
    received = []
    for piece in given:
        received.append(core_swap(piece))
    kept = call(
        functools.partial(gradient_kernel, plane_count, row_count),
        pair,
        (*slopes, voltage, adjoint),
        [VMEM] * 5,
    )
    summed, pieces = [], []
    for number in range(len(pair)):
        summed.append(kept[number] + received[number])
    for piece in summed:
        got = []
        for step in range(1, chips):
            got.append(chip_swap(piece[step], step))
        pieces.append(piece[0] + sum(got[1:], got[0]))
    predicted = pieces[-1][-SPARE, :pattern_count]
    pieces[-1] = pieces[-1][:-SPARE]
    bit = 1
    while bit < groups:
        for number in range(len(pieces)):
            pieces[number] = pieces[number] + swap(pieces[number], "pat", groups, bit)
        bit *= 2
    gradient = jnp.concatenate(pieces).reshape(plane_count, *plane)
    return gradient, predicted


def extended(block, sides, width):
    for axis, dim in sides:
        count = lax.axis_size(axis)
        forward = [(i, i + 1) for i in range(count - 1)]
        backward = [(target, source) for source, target in forward]
        low = lax.ppermute(
            lax.slice_in_dim(block, block.shape[dim] - width, None, axis=dim), axis, forward
        )
        high = lax.ppermute(lax.slice_in_dim(block, 0, width, axis=dim), axis, backward)
        block = jnp.concatenate([low, block, high], axis=dim)
    return block


def both_sides(values, along_axis):
    lower_pad = [(0, 0)] * values.ndim
    upper_pad = [(0, 0)] * values.ndim
    lower_pad[along_axis] = (1, 0)
    upper_pad[along_axis] = (0, 1)
    return jnp.pad(values, lower_pad) + jnp.pad(values, upper_pad)


def spread(values, along_axis):
    lower_pad = [(0, 0)] * values.ndim
    upper_pad = [(0, 0)] * values.ndim
    lower_pad[along_axis] = (1, 0)
    upper_pad[along_axis] = (0, 1)
    return jnp.pad(values, lower_pad) - jnp.pad(values, upper_pad)


def operate(values, coeffs):
    depth_faces, row_faces, column_faces = coeffs
    padded = extended(values, (("vox", 0),), 1)
    flux_depth = depth_faces[:, None] * (padded[1:] - padded[:-1])
    result = leakage * values + (flux_depth[:-1] - flux_depth[1:])
    result = result + spread(row_faces[:, None] * (values[:, :, 1:] - values[:, :, :-1]), 2)
    result = result + spread(
        column_faces[:, None] * (values[:, :, :, 1:] - values[:, :, :, :-1]), 3
    )
    return result


def inner(left_factor, right_factor):
    return jnp.sum(left_factor * right_factor, axis=(0, 2, 3))


def widen(vector):
    return vector[None, :, None, None]


def pattern_sum(local_terms):
    return lax.psum(local_terms, "vox")


def solve_pattern(right_side, initial, coeffs, diagonal):
    solution = initial
    residue = right_side - operate(solution, coeffs)
    precond = residue / diagonal
    direction = precond
    current = pattern_sum(inner(residue, precond))
    for iteration in range(ITERS):
        applied = operate(direction, coeffs)
        step_size = current / pattern_sum(inner(direction, applied))
        solution = solution + widen(step_size) * direction
        residue = residue - widen(step_size) * applied
        if iteration + 1 < ITERS:
            precond = residue / diagonal
            following = pattern_sum(inner(residue, precond))
            direction = precond + widen(following / current) * direction
            current = following
    return solution


def per_device_in_place(conductivity, warm_forward, warm_adjoint, electrodes, patterns, observed):
    plane_count, pattern_count, row_count, column_count = warm_forward.shape
    position = lax.axis_index("vox")
    layers = lax.axis_size("vox")
    strength = 2.0 * math.sqrt(layers * plane_count * row_count * column_count)
    data_weight = 0.1 * strength
    lower_open = (position > 0).astype(jnp.float32)
    upper_open = (position < layers - 1).astype(jnp.float32)
    padded_sigma = extended(conductivity, (("vox", 0),), 1)
    face_mask = jnp.concatenate(
        [lower_open[None], jnp.ones((plane_count - 1,), jnp.float32), upper_open[None]]
    )
    depth_faces = 0.5 * (padded_sigma[1:] + padded_sigma[:-1]) * face_mask[:, None, None]
    row_faces = 0.5 * (conductivity[:, 1:] + conductivity[:, :-1])
    column_faces = 0.5 * (conductivity[:, :, 1:] + conductivity[:, :, :-1])
    coeffs = (depth_faces, row_faces, column_faces)
    diagonal = (
        leakage
        + (depth_faces[:-1] + depth_faces[1:])
        + both_sides(row_faces, 1)
        + both_sides(column_faces, 2)
    )
    diagonal = diagonal[:, None]
    electrode_ids = jnp.arange(electrodes.shape[0], dtype=jnp.int32)
    picked = jnp.sum(
        jnp.where(
            patterns[:, :, None] == electrode_ids[None, None, :], electrodes[None, None, :], 0
        ),
        axis=2,
    )
    offset = position * (plane_count * row_count * column_count)
    local_cell = picked - offset
    grid_shape = (plane_count, 1, row_count, column_count)
    cell_index = (
        lax.broadcasted_iota(jnp.int32, grid_shape, 0) * row_count
        + lax.broadcasted_iota(jnp.int32, grid_shape, 2)
    ) * column_count + lax.broadcasted_iota(jnp.int32, grid_shape, 3)

    def marker(which_one):
        return (cell_index == local_cell[:, which_one][None, :, None, None]).astype(jnp.float32)

    forward = solve_pattern(strength * (marker(0) - marker(1)), warm_forward, coeffs, diagonal)
    probe_weights = marker(2) - marker(3)
    predicted = lax.psum(inner(probe_weights, forward), "vox")
    misfit = predicted - observed
    adjoint = solve_pattern(
        widen(data_weight * misfit) * probe_weights, warm_adjoint, coeffs, diagonal
    )
    stacked = jnp.concatenate([forward, adjoint], axis=1)
    padded_pair = extended(stacked, (("vox", 0),), 1)
    padded_forward = padded_pair[:, :pattern_count]
    padded_adjoint = padded_pair[:, pattern_count:]
    depth_products = jnp.sum(
        (padded_forward[1:] - padded_forward[:-1]) * (padded_adjoint[1:] - padded_adjoint[:-1]),
        axis=1,
    )
    depth_products = depth_products * face_mask[:, None, None]
    grad_depth = depth_products[:-1] + depth_products[1:]
    row_products = jnp.sum(
        (forward[:, :, 1:] - forward[:, :, :-1]) * (adjoint[:, :, 1:] - adjoint[:, :, :-1]), axis=1
    )
    column_products = jnp.sum(
        (forward[:, :, :, 1:] - forward[:, :, :, :-1])
        * (adjoint[:, :, :, 1:] - adjoint[:, :, :, :-1]),
        axis=1,
    )
    local_gradient = -0.5 * (
        grad_depth + both_sides(row_products, 1) + both_sides(column_products, 2)
    )
    gradient = lax.psum(local_gradient, "pat")
    return (gradient, predicted)


def per_device(conductivity, warm_forward, *rest):
    size = lax.axis_size("vox")
    groups = lax.axis_size("pat")
    exchange = warm_forward.shape[1] == size and size % CORES == 0
    exchange = exchange and size & (size - 1) == 0 and groups & (groups - 1) == 0
    form = per_device_exchanged if exchange else per_device_in_place
    return form(conductivity, warm_forward, *rest)


def solution(mesh):
    in_specs = (
        P("vox", None, None),
        P("vox", "pat", None, None),
        P("vox", "pat", None, None),
        P(),
        P("pat", None),
        P("pat"),
    )
    out_specs = (P("vox", None, None), P("pat"))
    return jax.shard_map(
        per_device, mesh=mesh, in_specs=in_specs, out_specs=out_specs, check_vma=False
    )
```

```python
import functools
import math

import jax
import jax.numpy as jnp
from jax import lax
from jax.experimental import pallas as pl
from jax.experimental.pallas import tpu as pltpu
from jax.sharding import PartitionSpec as P


ITERS = 2


leakage = 0.05

CORES = 2
SPARE = 8
ROWS = 256


VMEM = pl.BlockSpec(memory_space=pltpu.VMEM)
SMEM = pl.BlockSpec(memory_space=pltpu.SMEM)
HBM = pl.BlockSpec(memory_space=pltpu.HBM)


def call(body, out_shape, operands, in_specs, scratch=(), limit=1):
    moved = sum(4 * a.size for a in operands) + sum(4 * o.size for o in out_shape)
    return pl.pallas_call(
        body,
        out_shape=out_shape,
        in_specs=in_specs,
        out_specs=[VMEM] * len(out_shape),
        scratch_shapes=list(scratch),
        compiler_params=pltpu.CompilerParams(vmem_limit_bytes=limit << 20),
        cost_estimate=pl.CostEstimate(flops=moved, bytes_accessed=moved, transcendentals=0),
    )(*operands)


def shape(*dims):
    return jax.ShapeDtypeStruct(dims, jnp.float32)


def total(acc):
    return jnp.sum(acc, keepdims=True)


def fold(rows):
    return jnp.sum(rows.reshape(rows.shape[0] // 8, 8, rows.shape[1]), axis=0)


def ahead(rows):
    return pltpu.roll(rows, rows.shape[1] - 1, 1)


def behind(rows):
    return pltpu.roll(rows, 1, 1)


def padded(planes, height, width):
    return ((planes + 2) * height, width)


def clear_edges(*refs, height):
    for ref in refs:
        zero = jnp.zeros((height, ref.shape[1]), ref.dtype)
        ref[:height] = zero
        ref[ref.shape[0] - height :] = zero


def each_chunk(rows, height, body, start, size=ROWS):
    size = math.gcd(size, rows)

    def step(index, carry):
        base = pl.multiple_of(height + index * size, math.gcd(size, height))

        def at(ref, offset=0, value=None):
            where = pl.ds(base + offset, size)
            if value is None:
                return ref[where, :]
            ref[where, :] = value

        return body(at, index * size, carry)

    return lax.fori_loop(0, rows // size, step, start)


def neighbours(at, field, depth, rows, columns, height):
    here, column = at(field), at(columns)
    result = at(depth) * at(field, height) + at(depth, -height) * at(field, -height)
    result += at(rows) * at(field, 1)
    result += at(rows, -1) * at(field, -1)
    result += column * ahead(here) + behind(column * here)
    return here, result


def my_place():
    position = lax.axis_index("vox")
    return lax.div(position, CORES), lax.rem(position, CORES), position


def copy_all(pairs, sems):
    copies = [
        pltpu.make_async_copy(source, target, sems.at[number])
        for number, (source, target) in enumerate(pairs)
    ]
    for copy in copies:
        copy.start()
    for copy in copies:
        copy.wait()


def stage_kernel(share, conductivity, forward, fetched, *refs):
    chip = my_place()[0]
    size = fetched.shape[0]
    first = lax.rem(lax.axis_index("pat"), share) * size
    pairs = [(conductivity.at[pl.ds(first, size)], fetched)]
    for step, out in enumerate(refs[:-1], start=1):
        pairs.append((forward.at[:, pl.ds(CORES * (chip ^ step), CORES)], out))
    copy_all(pairs, refs[-1])


def stage_rest_kernel(forward, adjoint, kept, own, give, sems):
    chip, core, _ = my_place()
    pairs = [(forward.at[:, pl.ds(CORES * chip, CORES)], kept)]
    for plane in range(own.shape[0]):
        for other in range(own.shape[1]):
            pairs.append((adjoint.at[plane, CORES * other + 1 - core], give.at[plane, other]))
            pairs.append((adjoint.at[plane, CORES * other + core], own.at[plane, other]))
    copy_all(pairs, sems)


def pack_kernel(own, got, *outs):
    place = my_place()
    planes = own.shape[0]
    for step, out in enumerate(outs):
        other = place[0] ^ step
        for plane in range(planes):
            out[0, plane] = own[plane, other]
            out[1, plane] = got[plane, other]


def sort_kernel(*refs):
    place = my_place()
    blocks, keep, give = refs[:-2], refs[-2], refs[-1]
    for step, block in enumerate(blocks):
        for plane in range(block.shape[0]):
            keep[step, plane] = block[plane, place[1]]
            give[step, plane] = block[plane, 1 - place[1]]


def plane_rows(place, step, relative, plane, planes, height):
    level = ((place[0] ^ step) * CORES + (place[1] ^ relative)) * planes + plane
    return pl.ds(pl.multiple_of((level + 1) * height, height), height)


def coefficient_kernel(chips, share, own, others, depth, rows, columns, scale, root, sigma):
    place = my_place()
    total_planes, height, width = own.shape
    planes = total_planes // chips
    count = chips * CORES * planes
    part_planes = planes // share
    mine = lax.rem(lax.axis_index("pat"), share)
    clear_edges(depth, rows, columns, scale, root, sigma, height=height)
    fetched = [(0, plane) for plane in range(planes)]
    for half in range(share):
        owner = lax.rem(mine + half, share)
        for step in range(1, chips):
            fetched += [(step, owner * part_planes + plane) for plane in range(part_planes)]
    for relative, source in enumerate((own, others)):
        for number, (step, plane) in enumerate(fetched):
            sigma[plane_rows(place, step, relative, plane, planes, height), :] = source[number]
    row = lax.broadcasted_iota(jnp.int32, (height, width), 0)
    lane = lax.broadcasted_iota(jnp.int32, (height, width), 1)
    row_ahead, row_behind, lane_ahead = row < height - 1, row > 0, lane < width - 1

    def diagonals(at, first, carry):
        here = at(sigma)
        upper = jnp.where(first // height < count - 1, 0.5, 0.0) * (here + at(sigma, height))
        row_face = jnp.where(row_ahead, 0.5 * (here + at(sigma, 1)), 0.0)
        row_faces = row_face + jnp.where(row_behind, 0.5 * (here + at(sigma, -1)), 0.0)
        face = jnp.where(lane_ahead, 0.5 * (here + ahead(here)), 0.0)
        diagonal = leakage + (at(depth, -height) + upper) + row_faces + (behind(face) + face)
        inverse = lax.rsqrt(diagonal)
        inverse = inverse * (1.5 - 0.5 * diagonal * inverse * inverse)
        at(depth, value=upper)
        at(rows, value=row_face)
        at(columns, value=face)
        at(scale, value=inverse)
        at(root, value=diagonal * inverse)
        return carry

    each_chunk(count * height, height, diagonals, 0, height)

    def couplings(at, first, carry):
        size = at(scale)
        at(depth, value=at(depth) * (size * at(scale, height)))
        at(rows, value=at(rows) * (size * at(scale, 1)))
        at(columns, value=at(columns) * (size * ahead(size)))
        return carry

    each_chunk(count * height, height, couplings, 0)


def spot(ref, cell, height):
    width = ref.shape[1]
    lane = lax.broadcasted_iota(jnp.int32, (1, width), 1)
    return pl.ds(height + cell // width, 1), lane == cell % width


def add_at(ref, scale, cell, value, height):
    row, hit = spot(ref, cell, height)
    ref[row, :] += jnp.where(hit, value * scale[row, :], 0.0)


def value_at(ref, cell, height):
    row, hit = spot(ref, cell, height)
    return total(jnp.where(hit, ref[row, :], 0.0))


def solve_in_place(coefficients, sources, field, residue, applied, later, end, height):
    depth, rows, columns, scale = coefficients
    width = field.shape[1]
    size = field.shape[0] - 2 * height
    nothing = jnp.zeros((8, width), jnp.float32)
    clear_edges(field, residue, applied, height=height)

    def first(at, index, carry):
        here, sums = neighbours(at, field, depth, rows, columns, height)
        at(residue, value=sums - here)
        return carry

    each_chunk(size, height, first, 0)
    for cell, value in sources:
        add_at(residue, scale, cell, value, height)

    def second(at, index, carry):
        squares, products = carry
        here, sums = neighbours(at, residue, depth, rows, columns, height)
        product = here - sums
        at(applied, value=product)
        return squares + fold(here * here), products + fold(here * product)

    squares, products = each_chunk(size, height, second, (nothing, nothing), 2 * ROWS)
    current, energy = total(squares), total(products)
    step_size = current / energy

    def third(at, index, carry):
        squares, products, energies = carry

        def left(offset=0):
            return at(residue, offset) - step_size * at(applied, offset)

        here = left()
        at(later, value=here)
        sums = at(depth, -height) * left(-height) + at(rows, -1) * left(-1)
        sums += behind(at(columns) * here)
        squares = squares + fold(here * here)
        products = products + fold(here * at(applied))
        return squares, products, energies + fold(here * (here - 2.0 * sums))

    squares, products, energies = each_chunk(size, height, third, (nothing,) * 3, 2 * ROWS)
    following, cross, own = total(squares), total(products), total(energies)
    ratio = following / current
    last_size = following / (own + ratio * (2.0 * cross + ratio * energy))
    first_size = step_size + last_size * ratio

    def fifth(at, index, carry):
        moved = at(field) + first_size * at(residue) + last_size * at(later)
        end(at, at(scale) * moved)
        return carry

    each_chunk(size, height, fifth, 0, 2 * ROWS)


def electrode(place, electrodes, patterns, which):
    return electrodes[patterns[which, place[2]]]


def forward_kernel(strength, electrodes, patterns, *refs):
    place = my_place()
    depth, rows, columns, scale, root, own, others = refs[:7]
    *slopes, voltage, field, residue, applied, later, result = refs[7:]
    chips, planes, height, width = own.shape
    for step in range(chips):
        for relative, source in enumerate((own, others)):
            for plane in range(planes):
                where = plane_rows(place, step, relative, plane, planes, height)
                field[where, :] = source[step, plane] * root[where, :]
    plus, minus, high, low = (
        electrode(place, electrodes, patterns, which) for which in range(4)
    )

    def end(at, potential):
        at(result, value=potential)

    solve_in_place(
        (depth, rows, columns, scale),
        ((plus, strength), (minus, -strength)),
        field, residue, applied, later, end, height,
    )
    clear_edges(result, *slopes, height=height)
    count = chips * CORES * planes
    row = lax.broadcasted_iota(jnp.int32, (height, 1), 0)
    lane = lax.broadcasted_iota(jnp.int32, (1, width), 1)
    row_weight = jnp.where(row < height - 1, -0.5, 0.0)
    lane_weight = jnp.where(lane < width - 1, -0.5, 0.0)
    along_depth, along_row, along_column = slopes

    def slope(at, first, carry):
        here = at(result)
        depth_weight = jnp.where(first // height < count - 1, -0.5, 0.0)
        at(along_depth, value=depth_weight * (at(result, height) - here))
        at(along_row, value=row_weight * (at(result, 1) - here))
        at(along_column, value=lane_weight * (ahead(here) - here))
        return carry

    each_chunk(count * height, height, slope, 0, height)
    seen = value_at(result, high, height) - value_at(result, low, height)
    voltage[...] = jnp.broadcast_to(seen, voltage.shape)


def adjoint_kernel(weight, electrodes, patterns, observed, *refs):
    place = my_place()
    depth, rows, columns, scale, root, *slopes, voltage = refs[:9]
    *blocks, adjoint, given, last_given, field, residue, applied, later = refs[9:]
    planes, height, _ = blocks[0].shape[1:]
    for step, block in enumerate(blocks):
        for relative in range(CORES):
            for plane in range(planes):
                where = plane_rows(place, step, relative, plane, planes, height)
                field[where, :] = block[relative, plane] * root[where, :]
    weighted = weight * (voltage[0:1, :] - observed[place[2]])
    high = electrode(place, electrodes, patterns, 2)
    low = electrode(place, electrodes, patterns, 3)

    def end(at, potential):
        at(adjoint, value=potential)

    solve_in_place(
        (depth, rows, columns, scale),
        ((high, weighted), (low, -weighted)),
        field, residue, applied, later, end, height,
    )
    clear_edges(adjoint, height=height)
    gradient_pieces(place, 1, slopes, voltage, adjoint, (given, last_given), planes, height)


def gradient_kernel(planes, height, *refs):
    *slopes, voltage, adjoint, kept, last_kept = refs
    gradient_pieces(
        my_place(), 0, slopes, voltage, adjoint, (kept, last_kept), planes, height
    )


def gradient_pieces(place, relative, slopes, voltage, adjoint, outs, planes, height):
    along_depth, along_row, along_column = slopes
    chips, rows, width = outs[0].shape
    size = planes * height

    def step(block, carry):
        start = plane_rows(place, block, relative, 0, planes, height).start

        def at(ref, offset=0):
            return ref[pl.ds(start + offset, size), :]

        here = at(adjoint)
        result = at(along_depth) * (at(adjoint, height) - here)
        result += at(along_depth, -height) * (here - at(adjoint, -height))
        result += at(along_row) * (at(adjoint, 1) - here)
        result += at(along_row, -1) * (here - at(adjoint, -1))
        face = at(along_column) * (ahead(here) - here)
        result += face + behind(face)
        outs[0][block] = result[:rows]
        outs[1][block, : size - rows, :] = result[rows:]
        return carry

    lax.fori_loop(0, chips, step, 0)
    lane = lax.broadcasted_iota(jnp.int32, (SPARE, width), 1)
    note = jnp.where(lane == place[2], voltage[...], 0.0)
    for block in range(chips):
        outs[1][block, size - rows :, :] = note


def swap(values, axis, size, bit):
    return lax.ppermute(values, axis, [(i, i ^ bit) for i in range(size)])


def per_device_exchanged(
    conductivity, warm_forward, warm_adjoint, electrodes, patterns, observed
):
    plane_count, pattern_count, row_count, column_count = warm_forward.shape
    layers = lax.axis_size("vox")
    groups = lax.axis_size("pat")
    chips = layers // CORES
    strength = 2.0 * math.sqrt(layers * plane_count * row_count * column_count)
    plane = (row_count, column_count)
    whole = shape(*padded(layers * plane_count, *plane))
    room = pltpu.VMEM(whole.shape, jnp.float32)

    def chip_swap(values, step):
        return swap(values, "vox", layers, CORES * step)

    def core_swap(values):
        return swap(values, "vox", layers, 1)

    share = 2 if groups % 2 == 0 and plane_count % 2 == 0 else 1

    def in_place(values):
        return pltpu.with_memory_space_constraint(values, pltpu.HBM)

    fetched, *sends = call(
        functools.partial(stage_kernel, share),
        [shape(plane_count // share, *plane)]
        + [shape(plane_count, CORES, *plane)] * (chips - 1),
        (in_place(conductivity), in_place(warm_forward)),
        [HBM, HBM],
        scratch=[pltpu.SemaphoreType.DMA((chips,))],
    )
    sigma_got, blocks, adjoint_blocks = {}, {}, {}
    for step in range(1, chips):
        sigma_got[step] = chip_swap(fetched, step)
        blocks[step] = chip_swap(sends[step - 1], step)
    fetched = [sigma_got[step] for step in range(1, chips)]
    blocks[0], own, give = call(
        stage_rest_kernel,
        [shape(plane_count, CORES, *plane)] + [shape(plane_count, chips, *plane)] * 2,
        (in_place(warm_forward), in_place(warm_adjoint)),
        [HBM, HBM],
        scratch=[pltpu.SemaphoreType.DMA((1 + 2 * chips * plane_count,))],
    )
    blocks = [blocks[step] for step in range(chips)]
    got = core_swap(give)
    packed = call(
        pack_kernel, [shape(CORES, plane_count, *plane)] * chips, (own, got), [VMEM, VMEM]
    )
    adjoint_blocks[0] = packed[0]
    for step in range(1, chips):
        adjoint_blocks[step] = chip_swap(packed[step], step)
    adjoint_blocks = [adjoint_blocks[step] for step in range(chips)]
    others = [swap(jnp.concatenate(fetched), "pat", groups, 1)] if share == 2 else []
    own_sigma = jnp.concatenate([conductivity] + fetched + others)
    other_sigma = core_swap(own_sigma)
    coefficients = call(
        functools.partial(coefficient_kernel, chips, share),
        [whole] * 5,
        (own_sigma, other_sigma),
        [VMEM, VMEM],
        scratch=[room],
        limit=3,
    )
    keep, pass_on = call(
        sort_kernel, [shape(chips, plane_count, *plane)] * 2, tuple(blocks), [VMEM] * chips
    )
    received = core_swap(pass_on)
    *slopes, voltage = call(
        functools.partial(forward_kernel, strength),
        [whole] * 3 + [shape(SPARE, column_count)],
        (electrodes, patterns.T, *coefficients, keep, received),
        [SMEM] * 2 + [VMEM] * 7,
        scratch=[room] * 5,
        limit=8,
    )
    cut = (plane_count + 1) // 2 * row_count
    sizes = (cut, plane_count * row_count - cut + SPARE)
    pair = [shape(chips, size, column_count) for size in sizes]
    adjoint, *given = call(
        functools.partial(adjoint_kernel, 0.1 * strength),
        [whole] + pair,
        (
            electrodes, patterns.T, observed,
            *coefficients, *slopes, voltage, *adjoint_blocks,
        ),
        [SMEM] * 3 + [VMEM] * (9 + chips),
        scratch=[room] * 4,
        limit=8,
    )
    received = []
    for piece in given:
        received.append(core_swap(piece))
    kept = call(
        functools.partial(gradient_kernel, plane_count, row_count),
        pair,
        (*slopes, voltage, adjoint),
        [VMEM] * 5,
    )
    summed, pieces = [], []
    for number in range(len(pair)):
        summed.append(kept[number] + received[number])
    for piece in summed:
        got = []
        for step in range(1, chips):
            got.append(chip_swap(piece[step], step))
        pieces.append(piece[0] + sum(got[1:], got[0]))
    predicted = pieces[-1][-SPARE, :pattern_count]
    pieces[-1] = pieces[-1][:-SPARE]
    bit = 1
    while bit < groups:
        for number in range(len(pieces)):
            pieces[number] = pieces[number] + swap(pieces[number], "pat", groups, bit)
        bit *= 2
    gradient = jnp.concatenate(pieces).reshape(plane_count, *plane)
    return gradient, predicted


def extended(block, sides, width):
    for axis, dim in sides:
        count = lax.axis_size(axis)
        forward = [(i, i + 1) for i in range(count - 1)]
        backward = [(target, source) for source, target in forward]
        low = lax.ppermute(
            lax.slice_in_dim(block, block.shape[dim] - width, None, axis=dim), axis, forward
        )
        high = lax.ppermute(lax.slice_in_dim(block, 0, width, axis=dim), axis, backward)
        block = jnp.concatenate([low, block, high], axis=dim)
    return block


def both_sides(values, along_axis):
    lower_pad = [(0, 0)] * values.ndim
    upper_pad = [(0, 0)] * values.ndim
    lower_pad[along_axis] = (1, 0)
    upper_pad[along_axis] = (0, 1)
    return jnp.pad(values, lower_pad) + jnp.pad(values, upper_pad)


def spread(values, along_axis):
    lower_pad = [(0, 0)] * values.ndim
    upper_pad = [(0, 0)] * values.ndim
    lower_pad[along_axis] = (1, 0)
    upper_pad[along_axis] = (0, 1)
    return jnp.pad(values, lower_pad) - jnp.pad(values, upper_pad)


def operate(values, coeffs):
    depth_faces, row_faces, column_faces = coeffs
    padded = extended(values, (("vox", 0),), 1)
    flux_depth = depth_faces[:, None] * (padded[1:] - padded[:-1])
    result = leakage * values + (flux_depth[:-1] - flux_depth[1:])
    result = result + spread(row_faces[:, None] * (values[:, :, 1:] - values[:, :, :-1]), 2)
    result = result + spread(
        column_faces[:, None] * (values[:, :, :, 1:] - values[:, :, :, :-1]), 3
    )
    return result


def inner(left_factor, right_factor):
    return jnp.sum(left_factor * right_factor, axis=(0, 2, 3))


def widen(vector):
    return vector[None, :, None, None]


def pattern_sum(local_terms):
    return lax.psum(local_terms, "vox")


def solve_pattern(right_side, initial, coeffs, diagonal):
    solution = initial
    residue = right_side - operate(solution, coeffs)
    precond = residue / diagonal
    direction = precond
    current = pattern_sum(inner(residue, precond))
    for iteration in range(ITERS):
        applied = operate(direction, coeffs)
        step_size = current / pattern_sum(inner(direction, applied))
        solution = solution + widen(step_size) * direction
        residue = residue - widen(step_size) * applied
        if iteration + 1 < ITERS:
            precond = residue / diagonal
            following = pattern_sum(inner(residue, precond))
            direction = precond + widen(following / current) * direction
            current = following
    return solution


def per_device_in_place(conductivity, warm_forward, warm_adjoint, electrodes, patterns, observed):
    plane_count, pattern_count, row_count, column_count = warm_forward.shape
    position = lax.axis_index("vox")
    layers = lax.axis_size("vox")
    strength = 2.0 * math.sqrt(layers * plane_count * row_count * column_count)
    data_weight = 0.1 * strength
    lower_open = (position > 0).astype(jnp.float32)
    upper_open = (position < layers - 1).astype(jnp.float32)
    padded_sigma = extended(conductivity, (("vox", 0),), 1)
    face_mask = jnp.concatenate(
        [lower_open[None], jnp.ones((plane_count - 1,), jnp.float32), upper_open[None]]
    )
    depth_faces = 0.5 * (padded_sigma[1:] + padded_sigma[:-1]) * face_mask[:, None, None]
    row_faces = 0.5 * (conductivity[:, 1:] + conductivity[:, :-1])
    column_faces = 0.5 * (conductivity[:, :, 1:] + conductivity[:, :, :-1])
    coeffs = (depth_faces, row_faces, column_faces)
    diagonal = (
        leakage
        + (depth_faces[:-1] + depth_faces[1:])
        + both_sides(row_faces, 1)
        + both_sides(column_faces, 2)
    )
    diagonal = diagonal[:, None]
    electrode_ids = jnp.arange(electrodes.shape[0], dtype=jnp.int32)
    picked = jnp.sum(
        jnp.where(
            patterns[:, :, None] == electrode_ids[None, None, :], electrodes[None, None, :], 0
        ),
        axis=2,
    )
    offset = position * (plane_count * row_count * column_count)
    local_cell = picked - offset
    grid_shape = (plane_count, 1, row_count, column_count)
    cell_index = (
        lax.broadcasted_iota(jnp.int32, grid_shape, 0) * row_count
        + lax.broadcasted_iota(jnp.int32, grid_shape, 2)
    ) * column_count + lax.broadcasted_iota(jnp.int32, grid_shape, 3)

    def marker(which_one):
        return (cell_index == local_cell[:, which_one][None, :, None, None]).astype(jnp.float32)

    forward = solve_pattern(strength * (marker(0) - marker(1)), warm_forward, coeffs, diagonal)
    probe_weights = marker(2) - marker(3)
    predicted = lax.psum(inner(probe_weights, forward), "vox")
    misfit = predicted - observed
    adjoint = solve_pattern(
        widen(data_weight * misfit) * probe_weights, warm_adjoint, coeffs, diagonal
    )
    stacked = jnp.concatenate([forward, adjoint], axis=1)
    padded_pair = extended(stacked, (("vox", 0),), 1)
    padded_forward = padded_pair[:, :pattern_count]
    padded_adjoint = padded_pair[:, pattern_count:]
    depth_products = jnp.sum(
        (padded_forward[1:] - padded_forward[:-1]) * (padded_adjoint[1:] - padded_adjoint[:-1]),
        axis=1,
    )
    depth_products = depth_products * face_mask[:, None, None]
    grad_depth = depth_products[:-1] + depth_products[1:]
    row_products = jnp.sum(
        (forward[:, :, 1:] - forward[:, :, :-1]) * (adjoint[:, :, 1:] - adjoint[:, :, :-1]), axis=1
    )
    column_products = jnp.sum(
        (forward[:, :, :, 1:] - forward[:, :, :, :-1])
        * (adjoint[:, :, :, 1:] - adjoint[:, :, :, :-1]),
        axis=1,
    )
    local_gradient = -0.5 * (
        grad_depth + both_sides(row_products, 1) + both_sides(column_products, 2)
    )
    gradient = lax.psum(local_gradient, "pat")
    return (gradient, predicted)


def per_device(conductivity, warm_forward, *rest):
    size = lax.axis_size("vox")
    groups = lax.axis_size("pat")
    exchange = warm_forward.shape[1] == size and size % CORES == 0
    exchange = exchange and size & (size - 1) == 0 and groups & (groups - 1) == 0
    form = per_device_exchanged if exchange else per_device_in_place
    return form(conductivity, warm_forward, *rest)


def solution(mesh):
    in_specs = (
        P("vox", None, None),
        P("vox", "pat", None, None),
        P("vox", "pat", None, None),
        P(),
        P("pat", None),
        P("pat"),
    )
    out_specs = (P("vox", None, None), P("pat"))
    return jax.shard_map(
        per_device, mesh=mesh, in_specs=in_specs, out_specs=out_specs, check_vma=False
    )
```
